32 devices in a mesh: ctx: 4 (over x, core), fsdp: 4 (over z), rep: 2 (over y).
Axes of the slice: x: 2, y: 2, z: 4, core: 2. Of those that a mesh axis runs over, the one named last changes fastest.
Arguments:
- tokens: bfloat16 [8, 1024, 1024], P(('fsdp', 'rep'), 'ctx'), may hold values from -6 to 6
- segments: int32 [8, 1024], P(('fsdp', 'rep')), may hold values from 0 to 4, never falling along the last dimension, each value on 1 to 800 neighbouring positions
- ln1_gain: bfloat16 [1024], P(('ctx', 'fsdp')), may hold values from 0.5 to 1.5
- ln1_bias: bfloat16 [1024], P(('ctx', 'fsdp')), may hold values from -1 to 1
- w_qkv: bfloat16 [1024, 3072], P(('ctx', 'fsdp')), may hold values from -0.1875 to 0.1875
- q_bias: bfloat16 [1024], P(('ctx', 'fsdp')), may hold values from -1.5 to 1.5
- v_bias: bfloat16 [1024], P(('ctx', 'fsdp')), may hold values from -1.5 to 1.5
- w_out: bfloat16 [1024, 1024], P(('ctx', 'fsdp')), may hold values from -0.5 to 0.5
- out_bias: bfloat16 [1024], P(('ctx', 'fsdp')), may hold values from -1.5 to 1.5
- ln2_gain: bfloat16 [1024], P(('ctx', 'fsdp')), may hold values from 0.5 to 1.5
- ln2_bias: bfloat16 [1024], P(('ctx', 'fsdp')), may hold values from -1 to 1
- w_in: bfloat16 [1024, 4096], P(('ctx', 'fsdp')), may hold values from -0.1875 to 0.1875
- in_bias: bfloat16 [4096], P(('ctx', 'fsdp')), may hold values from -1.5 to 1.5
- w_back: bfloat16 [4096, 1024], P(('ctx', 'fsdp')), may hold values from -0.125 to 0.125
- back_bias: bfloat16 [1024], P(('ctx', 'fsdp')), may hold values from -1.5 to 1.5
- cotangent: bfloat16 [8, 1024, 1024], P(('fsdp', 'rep'), 'ctx'), may hold values from -6 to 6
Outputs:
- layer_output: bfloat16 [8, 1024, 1024], P(('fsdp', 'rep'), 'ctx')
- input_grad: float32 [8, 1024, 1024], P(('fsdp', 'rep'), 'ctx')
- ln1_gain_grad: float32 [1024], P(('ctx', 'fsdp'))
- ln1_bias_grad: float32 [1024], P(('ctx', 'fsdp'))
- w_qkv_grad: float32 [1024, 3072], P(('ctx', 'fsdp'))
- q_bias_grad: float32 [1024], P(('ctx', 'fsdp'))
- v_bias_grad: float32 [1024], P(('ctx', 'fsdp'))
- w_out_grad: float32 [1024, 1024], P(('ctx', 'fsdp'))
- out_bias_grad: float32 [1024], P(('ctx', 'fsdp'))
- ln2_gain_grad: float32 [1024], P(('ctx', 'fsdp'))
- ln2_bias_grad: float32 [1024], P(('ctx', 'fsdp'))
- w_in_grad: float32 [1024, 4096], P(('ctx', 'fsdp'))
- in_bias_grad: float32 [4096], P(('ctx', 'fsdp'))
- w_back_grad: float32 [4096, 1024], P(('ctx', 'fsdp'))
- back_bias_grad: float32 [1024], P(('ctx', 'fsdp'))
The draws below stay inside these ranges and needn't reach their ends.
Inputs may be any that keep to these rules, and one draw needn't show every extreme that they name: `segments`: segment numbers never fall along a sequence, every number of 0 to 4 occurs in each sequence, and some document of each sequence fills exactly 800 slots.
All inputs are finite; a program needn't handle non-finite values.
Results may differ from the reference program's by a relative error of at most 0.015.
Values may be sent and summed in bfloat16 or wider, within the bound.
A program may use at most 192 MiB of HBM per device.

```python
import math
import jax
import jax.numpy as jnp
import numpy as np
from jax import lax

D = 1024
H = 16
HD = 64
FF = 4096
SEQ = 1024
SEQS = 8
DOCS = 5
DOC_MOST = 800


def shard_levels(own_key, shape, cuts, least, largest):
    def one(dim, shards_of):
        steps = jax.random.uniform(jax.random.fold_in(jax.random.fold_in(own_key, 6), dim), (shards_of,), jnp.float32, least / len(cuts), largest / len(cuts))
        return jnp.repeat(jnp.exp(steps), shape[dim] // shards_of).reshape((-1,) + (1,) * (len(shape) - dim - 1))

    level = one(*cuts[0])
    for cut in cuts[1:]:
        level = level * one(*cut)
    return level


def split_up(number_of, total, bound, slope):
    portions = [(1 << 20) // math.isqrt(rank ** slope) + 1 for rank in range(2, number_of + 1)]
    surplus, given = total - bound - (number_of - 1), [1] * (number_of - 1)
    while surplus > 0:
        movable = [i for i in range(number_of - 1) if given[i] < bound]
        whole, remaining = sum([portions[i] for i in movable]), surplus
        for i in movable:
            addition = min(bound - given[i], max(1, remaining * portions[i] // whole), surplus)
            given[i] = given[i] + addition
            surplus = surplus - addition
    return np.array([bound] + given)


def uneven_parts(rng, number_of, total, bound, slope):
    if number_of == 2:
        one = jax.random.randint(rng, (), max(1, total - bound), min(bound, total - 1) + 1)
        return jnp.stack([one, total - one])
    lengths = jnp.asarray(split_up(number_of, total, bound, slope), jnp.int32)
    twos = (number_of - 1) // 2
    giver, sink = lengths[1:1 + 2 * twos:2], lengths[2:2 + 2 * twos:2]
    slack = jnp.minimum(giver - 1, bound - sink)
    passed = jax.random.randint(jax.random.fold_in(rng, 1), (twos,), 0, 1 << 20) % (slack + 1)
    lengths = lengths.at[1:1 + 2 * twos:2].set(giver - passed).at[2:2 + 2 * twos:2].set(sink + passed)
    return lengths[jax.random.permutation(jax.random.fold_in(rng, 2), number_of)]


def gaussian(stream_key, dims, deviation, limit, split=(), kind=jnp.bfloat16):
    level = shard_levels(stream_key, dims, split, -0.22, 0.18) if split else 1.0
    values = jax.random.normal(stream_key, dims, jnp.float32) * deviation * level
    return jnp.minimum(jnp.maximum(values, -limit), limit).astype(kind)


def setup_inputs(seed: int = 0) -> dict:
    splits = jax.random.split(jax.random.key(seed), 17)
    tokens = gaussian(splits[0], (SEQS, SEQ, D), 1.0, 6.0, ((0, 8), (1, 4)))
    segments = jax.vmap(lambda own: jnp.searchsorted(jnp.cumsum(uneven_parts(own, DOCS, SEQ, DOC_MOST, 1)), jnp.arange(SEQ), side="right"))(jax.random.split(splits[1], SEQS)).reshape((SEQS, SEQ)).astype(jnp.int32)
    ln1_gain = jnp.clip(1.0 + 0.1 * jax.random.normal(splits[2], (D,), jnp.float32), 0.5, 1.5).astype(jnp.bfloat16)
    ln1_bias = gaussian(splits[3], (D,), 0.2, 1.0, ((0, 16),))
    w_qkv = gaussian(splits[4], (D, 3 * D), D ** -0.5, 0.1875, ((0, 16),))
    q_bias = gaussian(splits[5], (D,), 0.3, 1.5, ((0, 16),))
    v_bias = gaussian(splits[6], (D,), 0.3, 1.5, ((0, 16),))
    w_out = gaussian(splits[7], (D, D), (D // 8) ** -0.5, 0.5, ((0, 16),))
    out_bias = gaussian(splits[8], (D,), 0.3, 1.5, ((0, 16),))
    ln2_gain = jnp.clip(1.0 + 0.1 * jax.random.normal(splits[9], (D,), jnp.float32), 0.5, 1.5).astype(jnp.bfloat16)
    ln2_bias = gaussian(splits[10], (D,), 0.2, 1.0, ((0, 16),))
    w_in = gaussian(splits[11], (D, FF), D ** -0.5, 0.1875, ((0, 16),))
    in_bias = gaussian(splits[12], (FF,), 0.3, 1.5, ((0, 16),))
    w_back = gaussian(splits[13], (FF, D), (FF // 2) ** -0.5, 0.125, ((0, 16),))
    back_bias = gaussian(splits[14], (D,), 0.3, 1.5, ((0, 16),))
    cotangent = gaussian(splits[15], (SEQS, SEQ, D), 1.0, 6.0, ((0, 8), (1, 4)))
    return dict(tokens=tokens, segments=segments, ln1_gain=ln1_gain, ln1_bias=ln1_bias, w_qkv=w_qkv, q_bias=q_bias, v_bias=v_bias, w_out=w_out, out_bias=out_bias, ln2_gain=ln2_gain, ln2_bias=ln2_bias, w_in=w_in, in_bias=in_bias, w_back=w_back, back_bias=back_bias, cotangent=cotangent)


@jax.custom_vjp
def low(v):
    return lax.optimization_barrier(v.astype(jnp.bfloat16)).astype(jnp.float32)

@jax.custom_vjp
def low_back(v):
    return v

def low_keep(v):
    return (low(v), None)

def low_pass(kept, grad):
    return (grad,)

def back_keep(v):
    return (v, None)

def back_low(kept, grad):
    return (low(grad),)
low.defvjp(low_keep, low_pass)
low_back.defvjp(back_keep, back_low)
epsilon = 1e-05
masked_value = -1e+30
highest = lax.Precision.HIGHEST

def rounded_both(values):
    return low(low_back(values))

def layer_norm(values, gain, shift):
    center = values - lax.optimization_barrier(jnp.mean(values, -1, keepdims=True))
    spread = lax.optimization_barrier(jnp.mean(center * center, -1, keepdims=True))
    return center * lax.rsqrt(spread + epsilon) * gain + shift

def forward(seq_x, seq_seg, weights):
    gain_one, shift_one, qkv_weight, query_bias, value_bias, proj_weight, proj_bias, gain_two, shift_two, up_weight, up_bias, down_weight, down_bias = weights
    length = seq_x.shape[0]
    width = seq_x.shape[1]
    normed_one = low(layer_norm(seq_x, gain_one, shift_one))
    projected = jnp.dot(normed_one, qkv_weight, precision=highest)
    queries = rounded_both(projected[:, :width] + query_bias).reshape(length, H, HD)
    key_rows = rounded_both(projected[:, width:2 * width]).reshape(length, H, HD)
    value_rows = rounded_both(projected[:, 2 * width:] + value_bias).reshape(length, H, HD)
    block_rows = min(512, length)
    block_count = length // block_rows
    query_blocks = queries.reshape(block_count, block_rows, H, HD)
    starts = jnp.arange(block_count, dtype=jnp.int32) * block_rows
    key_pos = jnp.arange(length, dtype=jnp.int32)
    score_scale = HD ** (-0.5)

    def attend(block_item):
        query_block, start = block_item
        query_pos = start + jnp.arange(block_rows, dtype=jnp.int32)
        query_seg = lax.dynamic_slice_in_dim(seq_seg, start, block_rows)
        scores = low_back(jnp.einsum('qhd,khd->hqk', query_block, key_rows, precision=highest) * score_scale)
        allowed = (query_seg[:, None] == seq_seg[None, :]) & (key_pos[None, :] <= query_pos[:, None])
        scores = jnp.where(allowed[None], scores, masked_value)
        probs = jax.nn.softmax(scores, axis=-1)
        return jnp.einsum('hqk,khd->qhd', low(probs), value_rows, precision=highest)
    attended = lax.map(jax.checkpoint(attend), (query_blocks, starts))
    attended = rounded_both(attended.reshape(length, width))
    branch = low_back(jnp.dot(attended, proj_weight, precision=highest) + proj_bias)
    resid = seq_x + branch
    normed_two = low(layer_norm(resid, gain_two, shift_two))
    pre_act = low_back(jnp.dot(normed_two, up_weight, precision=highest) + up_bias)
    activated = low(jax.nn.gelu(pre_act, approximate=True))
    mlp_branch = low_back(jnp.dot(activated, down_weight, precision=highest) + down_bias)
    return resid + mlp_branch

def reference(tokens, segments, ln1_gain, ln1_bias, w_qkv, q_bias, v_bias, w_out, out_bias, ln2_gain, ln2_bias, w_in, in_bias, w_back, back_bias, cotangent):
    weights = tuple((param.astype(jnp.float32) for param in (ln1_gain, ln1_bias, w_qkv, q_bias, v_bias, w_out, out_bias, ln2_gain, ln2_bias, w_in, in_bias, w_back, back_bias)))

    def seq_step(totals, seq_item):
        seq_x, seq_seg, seq_cot = seq_item
        result, pull_back = jax.vjp(lambda inputs, params: forward(inputs, seq_seg, params), seq_x.astype(jnp.float32), weights)
        input_grad, param_grads = pull_back(seq_cot.astype(jnp.float32))
        totals = tuple((total + grad for total, grad in zip(totals, param_grads)))
        return (totals, (result.astype(jnp.bfloat16), input_grad))
    initial = tuple((jnp.zeros(param.shape, jnp.float32) for param in weights))
    grads, (layer_output, input_grad) = lax.scan(seq_step, initial, (tokens, segments, cotangent))
    return (layer_output, input_grad, grads[0], grads[1], grads[2], grads[3], grads[4], grads[5], grads[6], grads[7], grads[8], grads[9], grads[10], grads[11], grads[12])
```

```python
import math

import jax
import jax.numpy as jnp
from jax import lax
from jax.sharding import PartitionSpec as P

H = 16
HD = 64
EPS = 1e-05
MASKED = -1e30
F32, BF16 = jnp.float32, jnp.bfloat16
OWN = ("ctx", "fsdp")


def dot(a, b, dims):
    return lax.dot_general(a, b, (dims, ((), ())), preferred_element_type=F32)


def norm_parts(x):
    center = x - jnp.mean(x, -1, keepdims=True)
    rstd = lax.rsqrt(jnp.mean(center * center, -1, keepdims=True) + EPS)
    return center * rstd, rstd


def norm_back(g, z, rstd, gain):
    gz = g * gain
    return rstd * (gz - jnp.mean(gz, -1, keepdims=True) - z * jnp.mean(gz * z, -1, keepdims=True))


def ctx_gather(x):
    return lax.all_gather(x, "ctx", axis=0, tiled=True)


def ctx_scatter(x):
    return lax.psum_scatter(x.astype(BF16), "ctx", scatter_dimension=0, tiled=True).astype(F32)


def shards(n, tokens, segments, ln1_gain, ln1_bias, w_qkv, q_bias, v_bias, w_out, out_bias,
           ln2_gain, ln2_bias, w_in, in_bias, w_back, back_bias, cotangent):
    own_rows, width = tokens.shape[1], tokens.shape[2]
    rows_in = w_qkv.shape[0]
    heads = H // n
    cols = heads * HD
    ctx = lax.axis_index("ctx")
    small = jnp.stack([ln1_gain, ln1_bias, q_bias, v_bias, out_bias, ln2_gain, ln2_bias, back_bias])
    small = lax.all_gather(small, OWN, axis=1, tiled=True).astype(F32)
    gain1, bias1, qb, vb, ob, gain2, bias2, bb = [small[i] for i in range(8)]
    qb = lax.dynamic_slice_in_dim(qb, ctx * cols, cols)
    vb = lax.dynamic_slice_in_dim(vb, ctx * cols, cols)
    inb = lax.all_gather(in_bias, "fsdp", axis=0, tiled=True).astype(F32)
    wq = lax.all_to_all(w_qkv.reshape(rows_in, 3, n, cols), "ctx", 2, 0)
    wq = lax.all_gather(wq.reshape(n, rows_in, 3 * cols), "fsdp", axis=1, tiled=True).reshape(width, 3 * cols)
    wo = lax.all_gather(w_out, "fsdp", axis=0, tiled=True)
    ffc = w_in.shape[1] // n
    wi = lax.all_to_all(w_in.reshape(rows_in, n, ffc), "ctx", 1, 0)
    wi = lax.all_gather(wi, "fsdp", axis=1, tiled=True).reshape(width, ffc)
    wb = lax.all_gather(w_back, "fsdp", axis=0, tiled=True)

    x = tokens[0].astype(F32)
    cot = cotangent[0]
    z1, rstd1 = norm_parts(x)
    n1 = ctx_gather((z1 * gain1 + bias1).astype(BF16))
    cot_all = ctx_gather(cot)
    proj = dot(n1, wq, ((1,), (0,)))
    slots = n1.shape[0]
    q = (proj[:, :cols] + qb).astype(BF16).reshape(slots, heads, HD)
    k = proj[:, cols:2 * cols].astype(BF16).reshape(slots, heads, HD)
    v = (proj[:, 2 * cols:] + vb).astype(BF16).reshape(slots, heads, HD)
    seg = segments[0]
    pos = jnp.arange(slots)
    allowed = ((seg[:, None] == seg[None, :]) & (pos[None, :] <= pos[:, None]))[None]
    scale = 1.0 / math.sqrt(HD)
    s = jnp.einsum("qhd,khd->hqk", q, k, preferred_element_type=F32)
    s = jnp.where(allowed, s * scale, MASKED)
    m = jnp.max(s, -1, keepdims=True)
    e = jnp.exp(s - m)
    probs = e / jnp.sum(e, -1, keepdims=True)
    pl_ = probs.astype(BF16)
    att = jnp.einsum("hqk,khd->qhd", pl_, v, preferred_element_type=F32).astype(BF16).reshape(slots, cols)
    resid = x + ctx_scatter(dot(att, wo, ((1,), (0,)))) + ob
    z2, rstd2 = norm_parts(resid)
    n2 = ctx_gather((z2 * gain2 + bias2).astype(BF16))
    pre = dot(n2, wi, ((1,), (0,))) + inb
    gelu = lambda t: jax.nn.gelu(t, approximate=True)
    act_f, pull = jax.vjp(gelu, pre)
    act = act_f.astype(BF16)
    g_pre = pull(dot(cot_all, wb, ((1,), (1,))))[0].astype(BF16)
    g_n2 = ctx_scatter(dot(g_pre, wi, ((1,), (1,))))
    out = resid + ctx_scatter(dot(act, wb, ((1,), (0,)))) + bb
    g_wb = dot(act, cot_all, ((0,), (0,)))
    g_wi = dot(n2, g_pre, ((0,), (0,)))
    g_inb = jnp.sum(g_pre, 0, dtype=F32)
    cot_f = cot.astype(F32)
    g_bb = jnp.sum(cot_f, 0)
    g_gain2, g_bias2 = jnp.sum(g_n2 * z2, 0), jnp.sum(g_n2, 0)
    g_resid = cot_f + norm_back(g_n2, z2, rstd2, gain2)
    gb_own = g_resid.astype(BF16)
    gb = ctx_gather(gb_own)
    g_ob = jnp.sum(gb_own, 0, dtype=F32)
    g_wo = dot(att, gb, ((0,), (0,)))
    g_att = dot(gb, wo, ((1,), (1,))).astype(BF16).reshape(slots, heads, HD)
    g_p = jnp.einsum("qhd,khd->hqk", g_att, v, preferred_element_type=F32)
    g_s = (probs * (g_p - jnp.sum(probs * g_p, -1, keepdims=True))).astype(BF16)
    g_q = (jnp.einsum("hqk,khd->qhd", g_s, k, preferred_element_type=F32) * scale).astype(BF16)
    g_k = (jnp.einsum("hqk,qhd->khd", g_s, q, preferred_element_type=F32) * scale).astype(BF16)
    g_v = jnp.einsum("hqk,qhd->khd", pl_, g_att, preferred_element_type=F32).astype(BF16)
    g_proj = jnp.concatenate([t.reshape(slots, cols) for t in (g_q, g_k, g_v)], 1)
    g_qb, g_vb = jnp.sum(g_proj[:, :cols], 0, dtype=F32), jnp.sum(g_proj[:, 2 * cols:], 0, dtype=F32)
    g_n1 = ctx_scatter(dot(g_proj, wq, ((1,), (1,))))
    g_wq = dot(n1, g_proj, ((0,), (0,)))
    g_gain1, g_bias1 = jnp.sum(g_n1 * z1, 0), jnp.sum(g_n1, 0)
    g_x = g_resid + norm_back(g_n1, z1, rstd1, gain1)

    def owners(g):
        return lax.psum_scatter(g.astype(BF16), "fsdp", scatter_dimension=0, tiled=True)

    def by_rows(g, parts):
        g = g.astype(BF16).reshape(n, -1, g.shape[1])
        g = lax.psum_scatter(g, "fsdp", scatter_dimension=1, tiled=True)
        g = lax.all_to_all(g, "ctx", 0, 0)
        g = g.reshape(n, rows_in, parts, -1).transpose(1, 2, 0, 3)
        return g.reshape(rows_in, -1)

    grads = [by_rows(g_wq, 3), owners(g_wo), by_rows(g_wi, 1), owners(g_wb)]
    grads = [lax.psum(g, "rep").astype(F32) for g in grads]
    spread = lambda g: lax.dynamic_update_slice_in_dim(jnp.zeros((width,), F32), g, ctx * cols, 0)
    vec = jnp.stack([g_gain1, g_bias1, spread(g_qb), spread(g_vb), g_ob, g_gain2, g_bias2, g_bb])
    vec = lax.psum(lax.psum_scatter(vec, OWN, scatter_dimension=1, tiled=True), "rep")
    g_inb = lax.psum(lax.psum_scatter(g_inb, "fsdp", scatter_dimension=0, tiled=True), "rep")
    return (out.astype(BF16)[None], g_x[None], vec[0], vec[1], grads[0], vec[2], vec[3], grads[1],
            vec[4], vec[5], vec[6], grads[2], g_inb, grads[3], vec[7])


def solution(mesh):
    own, rows = P(OWN), P(OWN, None)
    seqs = P(("fsdp", "rep"), "ctx", None)
    in_specs = (seqs, P(("fsdp", "rep"), None), own, own, rows, own, own, rows, own, own, own, rows, own, rows, own, seqs)
    out_specs = (seqs, seqs, own, own, rows, own, own, rows, own, own, own, rows, own, rows, own)
    n = mesh.shape["ctx"]
    body = lambda *args: shards(n, *args)
    return jax.shard_map(body, mesh=mesh, in_specs=in_specs, out_specs=out_specs, check_vma=False)
```

```python
import functools

import jax
import jax.numpy as jnp
from jax import lax
from jax.experimental import pallas as pl
from jax.experimental.pallas import tpu as pltpu
from jax.sharding import PartitionSpec as P

H = 16
HD = 64
DOCS = 5
EPS = 1e-05
MASKED = -1e30
F32, BF16 = jnp.float32, jnp.bfloat16
MESH = pl.DeviceIdType.MESH
NN = ((1,), (0,))
NT = ((1,), (1,))
TN = ((0,), (0,))
QKV, OUT, IN, BACK = range(4)
CHUNK = 32


def dot(a, b, dims):
    return lax.dot_general(a, b, (dims, ((), ())), preferred_element_type=F32)


def norm_parts(x):
    center = x - jnp.mean(x, -1, keepdims=True)
    rstd = lax.rsqrt(jnp.mean(center * center, -1, keepdims=True) + EPS)
    return center * rstd, rstd


def norm_back(g, z, rstd, gain):
    gz = g * gain
    return rstd * (gz - jnp.mean(gz, -1, keepdims=True) - z * jnp.mean(gz * z, -1, keepdims=True))


def gelu_both(t):
    a, b = 0.7978845608028654, 0.044715
    t2 = t * t
    th = jnp.tanh(a * t * (1.0 + b * t2))
    half = 0.5 * (1.0 + th)
    return t * half, half + 0.5 * t * (1.0 - th * th) * (a * (1.0 + 3.0 * b * t2))


def fold(x):
    return jnp.sum(x.reshape(x.shape[0] // 8, 8, x.shape[1]), 0)


def body(dims, tok, cot_in, seg, pack, wq_hbm, wo_hbm, wi_hbm, wb_hbm,
         out_o, gx_o, gq_o, go_o, gi_o, gb_o, gv_o,
         wq, wo, wi, wb, packs, vecs, inb, n1, cot, n2, gbr, q_s, k_s, v_s, do_s, kt_s, vt_s, att, act, gpre, gproj,
         start_s, lse_s, delta_s, resid, gres, keep, tmp1, tmp2, snd, land,
         dk_s, dv_s, gwq, gwo, gwi, gwb, yq, yo, yi, yb, zq, zo, zi, zb, fq, fi, aq, ao, ai, ab,
         v6, v6r, vs, vy, vs2, vz, ibg, sums,
         loc, pk_cs, pk_cr, pk_zs, pk_zr, wc_s, wc_r, wz_s, wz_r, wy_s, wy_r, ag_s, ag_r, rs_s, rs_r,
         gy_s, gy_r, gz_s, gz_r, gc_s, gc_r, gf_s, gf_r, vc_s, vc_r, vy_s, vy_r, vz_s, vz_r):
    n, nf, t_rows, width, rows, brows, ffc = dims
    half_w, half_f = width // 2, ffc // 2
    hc = width // n
    pw = hc // 2
    c, f, r = lax.axis_index("ctx"), lax.axis_index("fsdp"), lax.axis_index("rep")
    x, core = c // 2, c % 2

    def rel(d):
        return ((x + d // 2) % 2) * 2 + (core + d % 2) % 2

    def on_ctx(d):
        return (rel(d), f, r)

    def on_z(f2):
        return (c, f2, r)

    on_y = (c, f, 1 - r)
    ends = []

    def make(src, dst, ss, rs, dev):
        return pltpu.make_async_remote_copy(src_ref=src, dst_ref=dst, send_sem=ss, recv_sem=rs, device_id=dev,
                                            device_id_type=MESH)

    def send(src, dst, ss, rs, dev, cond=None):
        if cond is None:
            make(src, dst, ss, rs, dev).start()
            ends.append(lambda: make(src, dst, ss, rs, dev).wait_send())
        else:
            @pl.when(cond)
            def _():
                make(src, dst, ss, rs, dev).start()

            def end():
                @pl.when(cond)
                def _():
                    make(src, dst, ss, rs, dev).wait_send()
            ends.append(end)

    def arrived(dst, rs, dev):
        make(dst, dst, rs, rs, dev).wait_recv()

    def local(src, dst, sem):
        pltpu.make_async_copy(src, dst, sem).start()

    def local_done(dst, sem):
        pltpu.make_async_copy(dst, dst, sem).wait()

    local(cot_in, cot.at[c], loc.at[0])
    for h in range(2):
        for j in range(3):
            local(wq_hbm.at[:, pl.ds(pl.multiple_of(j * width + c * hc + h * pw, pw), pw)],
                  wq.at[h, c, f, :, pl.ds(j * pw, pw)], loc.at[1])
        local(wo_hbm.at[:, pl.ds(h * half_w, half_w)], wo.at[h, f], loc.at[2])
        local(wi_hbm.at[:, pl.ds(pl.multiple_of(c * ffc + h * half_f, half_f), half_f)], wi.at[h, c, f], loc.at[3])
        local(wb_hbm.at[:, pl.ds(h * half_w, half_w)], wb.at[h, f], loc.at[4])
    packs[c, f] = pack[...]
    barrier = pltpu.get_barrier_semaphore()
    peers = [on_ctx(d) for d in (1, 2, 3)] + [on_z((f + s) % nf) for s in range(1, nf)] + [on_y]
    for dev in peers:
        pl.semaphore_signal(barrier, inc=1, device_id=dev, device_id_type=MESH)
    pl.semaphore_wait(barrier, len(peers))

    for d in (1, 2, 3):
        send(packs.at[c, f], packs.at[c, f], pk_cs.at[d], pk_cr.at[c], on_ctx(d))

    def exchange(kind, hbm, buf, parts, step, w):
        for d in (2, 3, 1):
            c2 = rel(d)
            for h in range(2):
                for j in range(parts):
                    make(hbm.at[:, pl.ds(pl.multiple_of(j * width + c2 * step + h * w, w), w)],
                         buf.at[h, c, f, :, pl.ds(j * w, w)], wc_s.at[kind, d], wc_r.at[kind, c], on_ctx(d)).start()
            ends.append(lambda d=d: make(buf.at[:, c, f], buf.at[:, c, f], wc_s.at[kind, d], wc_r.at[kind, c],
                                         on_ctx(d)).wait_send())

    def exchanged(kind, buf):
        for d in (1, 2, 3):
            arrived(buf.at[:, rel(d), f], wc_r.at[kind, rel(d)], on_ctx(d))

    exchange(0, wq_hbm, wq, 3, hc, pw)

    bufs = {QKV: wq, OUT: wo, IN: wi, BACK: wb}

    def block(buf, kind, h, f2):
        return buf.at[h, :, f2] if kind in (QKV, IN) else buf.at[h, f2]

    def w_send(kind, way, src, cond):
        nxt = f + 1 if way == 0 else f - 1
        b = block(bufs[kind], kind, r, src)
        send(b, b, wz_s.at[kind, way, src], wz_r.at[kind, src], on_z(nxt), cond)

    def w_own(kind):
        w_send(kind, 0, f, f + 1 < nf)
        w_send(kind, 1, f, f >= 1)

    def w_step(kind, s):
        for way in range(2):
            src = f - s if way == 0 else f + s
            ok = src >= 0 if way == 0 else src < nf
            b = block(bufs[kind], kind, r, src)

            @pl.when(ok)
            def _():
                arrived(b, wz_r.at[kind, src], on_y)
            w_send(kind, way, src, ok & ((f + 1 < nf) if way == 0 else (f >= 1)))
            send(b, b, wy_s.at[kind, src], wy_r.at[kind, src], on_y, ok)

    def w_arrived(kind):
        for s in range(1, nf):
            f2 = (f + s) % nf
            arrived(block(bufs[kind], kind, 1 - r, f2), wy_r.at[kind, f2], on_y)

    def ag_start(i, buf):
        for d, k in ((2, 0), (1, 1)):
            send(buf.at[c], buf.at[c], ag_s.at[i, k], ag_r.at[i, c], on_ctx(d))

    def ag_forward(i, buf):
        b = rel(2)
        arrived(buf.at[b], ag_r.at[i, b], on_ctx(2))
        send(buf.at[b], buf.at[b], ag_s.at[i, 2], ag_r.at[i, b], on_ctx(1))

    def ag_wait(i, buf, d):
        arrived(buf.at[rel(d)], ag_r.at[i, rel(d)], on_ctx(d))

    def rs_put(i, d, h, val):
        cols = pl.ds(h * half_w, half_w)
        if d == 0:
            keep[:, cols] = val
            return
        k = {3: 0, 2: 1, 1: 2}[d]
        if d == 2:
            arrived(land.at[i, 0, h], rs_r.at[i, 0, h], on_ctx(1))
            val = val + land[i, 0, h].astype(F32)
        snd[i % 2, k, h] = val.astype(BF16)
        make(snd.at[i % 2, k, h], land.at[i, k, h], rs_s.at[i, k, h], rs_r.at[i, k, h], on_ctx(2 if d == 2 else 1)).start()

    def rs_sent(i):
        for d, k in ((3, 0), (2, 1), (1, 2)):
            for h in range(2):
                make(snd.at[i % 2, k, h], land.at[i, k, h], rs_s.at[i, k, h], rs_r.at[i, k, h],
                     on_ctx(2 if d == 2 else 1)).wait_send()

    def rs_arrived(i):
        for h in range(2):
            arrived(land.at[i, 2, h], rs_r.at[i, 2, h], on_ctx(1))
            arrived(land.at[i, 1, h], rs_r.at[i, 1, h], on_ctx(2))

    def rs_rows(i, rw):
        parts = [keep[rw, pl.ds(h * half_w, half_w)] + land[i, 1, h, rw].astype(F32) + land[i, 2, h, rw].astype(F32)
                 for h in range(2)]
        return jnp.concatenate(parts, 1)

    def chunks(fn, init=0, size=CHUNK):
        return lax.fori_loop(0, t_rows // size, lambda i, v: fn(pl.ds(pl.multiple_of(i * size, size), size), v), init)

    sg = seg[...]
    start = jnp.zeros_like(sg)
    for doc in range(DOCS - 1):
        start = start + jnp.where(sg > doc, jnp.sum((sg == doc).astype(jnp.int32), -1, keepdims=True), 0)
    for b in range(n):
        start_s[b] = start[:, b * t_rows:(b + 1) * t_rows]

    for d in (1, 2, 3):
        arrived(packs.at[rel(d), f], pk_cr.at[rel(d)], on_ctx(d))
    for s in range(1, nf):
        f2 = (f + s) % nf
        send(packs.at[:, f], packs.at[:, f], pk_zs.at[s], pk_zr.at[f], on_z(f2))
    local_done(wq.at[:, c, f], loc.at[1])
    exchanged(0, wq)
    w_own(QKV)
    for s in range(1, nf):
        f2 = (f + s) % nf
        arrived(packs.at[:, f2], pk_zr.at[f2], on_z(f2))
    lane = lax.broadcasted_iota(jnp.int32, (8, 128), 1)
    per = 128 // rows
    for g in range(width // 128):
        acc = None
        for j in range(per):
            e = g * per + j
            piece = packs[e // nf, e % nf].astype(F32)[0:8]
            acc = piece if j == 0 else jnp.where(lane // rows == j, pltpu.roll(piece, j * rows, 1), acc)
        vecs[g] = acc
    for g in range(ffc // 128):
        acc = None
        for j in range(per):
            e = g * per + j
            k = e % 4
            piece = packs[c, e // 4].astype(F32)[8:16]
            piece = jnp.broadcast_to(piece[k:k + 1], (8, 128))
            acc = piece if j == 0 else jnp.where(lane // rows == j, pltpu.roll(piece, j * rows, 1), acc)
        inb[:, g * 128:(g + 1) * 128] = acc

    def vec(v):
        return jnp.concatenate([vecs[g, v:v + 1, :] for g in range(width // 128)], 1)

    def ln1(rw, _):
        z, _r = norm_parts(tok[rw].astype(F32))
        n1[c, rw] = (z * vec(0) + vec(1)).astype(BF16)
        return 0
    chunks(ln1)
    ag_start(0, n1)
    exchange(1, wi_hbm, wi, 1, ffc, half_f)
    local_done(cot.at[c], loc.at[0])
    ag_start(1, cot)
    local_done(wo.at[:, f], loc.at[2])
    for s in range(1, nf):
        w_step(QKV, s)
        if s == 1:
            w_own(OUT)
    ag_forward(0, n1)
    local_done(wi.at[:, c, f], loc.at[3])
    exchanged(1, wi)
    w_own(IN)
    for s in range(1, nf):
        w_step(OUT, s)
    ag_wait(0, n1, 1)
    ag_wait(0, n1, 3)
    w_arrived(QKV)

    def project(b, _):
        for p in range(2):
            pr = dot(n1[b], wq[p].reshape(width, 3 * pw), NN)
            qv = ((pr[:, :pw] + vecs[c * 2 + p, 2:3, :]).astype(BF16).astype(F32) * (HD ** -0.5)).astype(BF16)
            kv = pr[:, pw:2 * pw].astype(BF16)
            vv = (pr[:, 2 * pw:] + vecs[c * 2 + p, 3:4, :]).astype(BF16)
            kt, vt = kv.T, vv.T
            for e in range(2):
                q_s[2 * p + e, b] = qv[:, e * HD:(e + 1) * HD]
                k_s[2 * p + e, b] = kv[:, e * HD:(e + 1) * HD]
                v_s[2 * p + e, b] = vv[:, e * HD:(e + 1) * HD]
                kt_s[2 * p + e, b] = kt[e * HD:(e + 1) * HD]
                vt_s[2 * p + e, b] = vt[e * HD:(e + 1) * HD]
        return 0
    lax.fori_loop(0, n, project, 0)

    key_row = lax.broadcasted_iota(jnp.int32, (t_rows, t_rows), 0)
    query_col = lax.broadcasted_iota(jnp.int32, (t_rows, t_rows), 1)

    def scores(h, qb, kb, diagonal):
        s = dot(k_s[h, kb], q_s[h, qb], NT)
        ok = key_row >= start_s[qb] - kb * t_rows
        if diagonal:
            ok = ok & (key_row <= query_col)
        return jnp.where(ok, s, MASKED)

    def attend(h, qb):
        def step(kb, carry, diagonal=False):
            m, l, acc = carry
            s = scores(h, qb, kb, diagonal)
            m2 = jnp.maximum(m, jnp.max(s, 0, keepdims=True))
            p = jnp.exp(s - m2)
            a = jnp.exp(m - m2)
            return m2, l * a + jnp.sum(p, 0, keepdims=True), acc * a + dot(vt_s[h, kb], p.astype(BF16), NN)
        zero = jnp.zeros((1, t_rows), F32)
        carry = lax.fori_loop(0, qb, step, (zero + MASKED, zero, jnp.zeros((HD, t_rows), F32)))
        m, l, acc = step(qb, carry, True)
        att[qb, h] = (acc / l).astype(BF16)
        lse_s[h, qb] = m + jnp.log(l)

    for d in (3, 2, 1, 0):
        qb = rel(d)

        def heads(h, _):
            attend(h, qb)
            return 0
        lax.fori_loop(0, H // n, heads, 0)
        if d == 3:
            w_arrived(OUT)
            local_done(wb.at[:, f], loc.at[4])
            w_own(BACK)
        if 4 - d < nf:
            w_step(IN, 4 - d)
        for h in range(2):
            rs_put(0, d, h, dot(att[qb].reshape(hc, t_rows), wo[h].reshape(hc, half_w), TN))
    for s in range(5, nf):
        w_step(IN, s)
    ag_forward(1, cot)
    rs_arrived(0)

    def ln2(rw, _):
        res = tok[rw].astype(F32) + rs_rows(0, rw) + vec(4)
        resid[rw] = res
        z, _r = norm_parts(res)
        n2[c, rw] = (z * vec(5) + vec(6)).astype(BF16)
        return 0
    chunks(ln2)
    ag_start(2, n2)
    for s in range(1, nf):
        w_step(BACK, s)
    w_arrived(IN)
    ag_wait(1, cot, 1)
    ag_wait(1, cot, 3)
    w_arrived(BACK)

    ibg[...] = jnp.zeros_like(ibg)
    for d in (0, 1, 3, 2):
        b = rel(d)
        if d == 1:
            ag_wait(2, n2, 1)
        if d == 3:
            ag_forward(2, n2)
            ag_wait(2, n2, 3)

        def up(j, _):
            tmp1[...] = dot(n2[b], wi[j].reshape(width, half_f), NN)
            wide = jnp.concatenate([wb[h, pl.ds(j * (nf // 2), nf // 2)].reshape(half_f, half_w) for h in range(2)], 1)
            tmp2[...] = dot(cot[b], wide, NT)
            bias = inb[0:1, pl.ds(pl.multiple_of(j * half_f, half_f), half_f)]
            cols = pl.ds(pl.multiple_of(j * half_f, half_f), half_f)

            def one(rw, acc):
                a, da = gelu_both(tmp1[rw] + bias)
                act[b, rw, cols] = a.astype(BF16)
                gp = (tmp2[rw] * da).astype(BF16)
                gpre[b, rw, cols] = gp
                return acc + fold(gp.astype(F32))
            ibg[j] += chunks(one, jnp.zeros((8, half_f), F32))
            return 0
        lax.fori_loop(0, 2, up, 0)
        if d == 3:
            rs_sent(0)
        for h in range(2):
            wide = jnp.concatenate([wi[j, pl.ds(h * (n // 2), n // 2)].reshape(half_w, half_f) for j in range(2)], 1)
            rs_put(1, d, h, dot(gpre[b], wide, NT))

    grads = {QKV: (gwq, yq, zq), OUT: (gwo, yo, zo), IN: (gwi, yi, zi), BACK: (gwb, yb, zb)}
    alls = {QKV: aq, OUT: ao, IN: ai, BACK: ab}

    def g_y(kind):
        g, y, _z = grads[kind]
        send(g.at[1 - r], y, gy_s.at[kind], gy_r.at[kind], on_y)

    def g_z(kind):
        g, y, z = grads[kind]
        arrived(y, gy_r.at[kind], on_y)

        def add(i, _):
            g[r, i] = (g[r, i].astype(F32) + y[i].astype(F32)).astype(BF16)
            return 0
        lax.fori_loop(0, y.shape[0], add, 0)
        for s in range(1, nf):
            f2 = (f + s) % nf
            send(block(g, kind, r, f2), z.at[f], gz_s.at[kind, s], gz_r.at[kind, f], on_z(f2))

    def g_f(kind):
        g, _y, z = grads[kind]
        for s in range(1, nf):
            f2 = (f + s) % nf
            arrived(z.at[f2], gz_r.at[kind, f2], on_z(f2))
        if kind in (QKV, IN):
            fin, k = (fq, 0) if kind == QKV else (fi, 1)

            def add(i, _):
                tot = g[r, i, f].astype(F32)
                for s in range(1, nf):
                    tot = tot + z[(f + s) % nf, i].astype(F32)
                fin[i] = tot.astype(BF16)
                return 0
            lax.fori_loop(0, n, add, 0)
            for d in (2, 3, 1):
                send(fin.at[rel(d)], alls[kind].at[r, c], gc_s.at[k, d], gc_r.at[k, c], on_ctx(d))
            alls[kind][r, c] = fin[c]
        else:
            tot = g[r, f].astype(F32)
            for s in range(1, nf):
                tot = tot + z[(f + s) % nf].astype(F32)
            alls[kind][r] = tot.astype(BF16)
            send(alls[kind].at[r], alls[kind].at[r], gf_s.at[kind], gf_r.at[kind], on_y)

    def g_e(kind):
        k = 0 if kind == QKV else 1
        a = alls[kind]
        for d in (1, 2, 3):
            arrived(a.at[r, rel(d)], gc_r.at[k, rel(d)], on_ctx(d))
        send(a.at[r], a.at[r], gf_s.at[kind], gf_r.at[kind], on_y)

    def g_out(kind):
        a = alls[kind]
        arrived(a.at[1 - r], gf_r.at[kind], on_y)
        for h in range(2):
            if kind == OUT:
                go_o[:, h * half_w:(h + 1) * half_w] = ao[h].astype(F32)
            elif kind == BACK:
                gb_o[:, h * half_w:(h + 1) * half_w] = ab[h].astype(F32)
            else:
                for c2 in range(n):
                    if kind == IN:
                        gi_o[:, c2 * ffc + h * half_f:c2 * ffc + (h + 1) * half_f] = ai[h, c2].astype(F32)
                    else:
                        for j in range(3):
                            lo = j * width + c2 * hc + h * pw
                            gq_o[:, lo:lo + pw] = aq[h, c2, :, j * pw:(j + 1) * pw].astype(F32)

    def whole(buf, cols):
        v = buf[:, :, cols]
        return v.reshape(n * t_rows, v.shape[2])

    def grad_back(h):
        per_f = ffc // nf
        tiles = max(1, 256 // per_f)

        def one(i, _):
            a = whole(act, pl.ds(pl.multiple_of(i * 256, 256), 256))
            g = whole(cot, pl.ds(pl.multiple_of(h * half_w, half_w), half_w))
            v = dot(a, g, TN).astype(BF16)
            gwb[h, pl.ds(i * tiles, tiles)] = v.reshape(tiles, per_f, half_w)
            return 0
        lax.fori_loop(0, ffc // 256, one, 0)

    def grad_in(h):
        def one(i, _):
            a = whole(n2, pl.ds(pl.multiple_of(i * hc, hc), hc))
            g = whole(gpre, pl.ds(pl.multiple_of(h * half_f, half_f), half_f))
            gwi[h, i] = dot(a, g, TN).astype(BF16).reshape(nf, rows, half_f)
            return 0
        lax.fori_loop(0, n, one, 0)

    grad_back(1 - r)
    g_y(BACK)
    grad_back(r)
    rs_arrived(1)

    def ln2_back(rw, accs):
        gain, shift, bb, ob = accs
        g = rs_rows(1, rw)
        z, rstd = norm_parts(resid[rw])
        ct = cot[c, rw].astype(F32)
        gr = ct + norm_back(g, z, rstd, vec(5))
        gres[rw] = gr
        low = gr.astype(BF16)
        gbr[c, rw] = low
        return gain + fold(g * z), shift + fold(g), bb + fold(ct), ob + fold(low.astype(F32))
    zero8 = jnp.zeros((8, width), F32)
    accs = chunks(ln2_back, (zero8, zero8, zero8, zero8), 16)
    for i, a in zip((3, 4, 5, 2), accs):
        sums[i] = a
    ag_start(3, gbr)
    grad_in(1 - r)
    g_y(IN)
    grad_in(r)
    g_z(BACK)
    ag_forward(3, gbr)

    for d in (3, 2, 1, 0):
        for h in range(2):
            rs_put(2, d, h, dot(act[rel(d)], wb[h].reshape(ffc, half_w), NN))
    ag_wait(3, gbr, 1)
    ag_wait(3, gbr, 3)

    def g_attended(b, _):
        wide = jnp.concatenate([wo[h].reshape(hc, half_w) for h in range(2)], 1)
        g = dot(gbr[b], wide, NT).astype(BF16)
        gt = g.T.astype(F32).reshape(H // n, HD, t_rows)
        for h in range(H // n):
            do_s[h, b] = g[:, h * HD:(h + 1) * HD]
            delta_s[h, b] = jnp.sum(gt[h] * att[b, h].astype(F32), 0, keepdims=True)
        return 0
    lax.fori_loop(0, n, g_attended, 0)
    g_z(IN)

    def grad_out(h):
        tot = jnp.zeros((hc, half_w), F32)
        cols = pl.ds(pl.multiple_of(h * half_w, half_w), half_w)
        for b in range(n):
            tot = tot + dot(att[b].reshape(hc, t_rows), gbr[b, :, cols], NN)
        gwo[h] = tot.astype(BF16).reshape(nf, rows, half_w)
    grad_out(1 - r)
    g_y(OUT)
    grad_out(r)

    rs_arrived(2)

    def finish_out(rw, _):
        out_o[rw] = (resid[rw] + rs_rows(2, rw) + vec(7)).astype(BF16)
        return 0
    chunks(finish_out)

    def attend_back(h, e, p, qb):
        q, do = q_s[h, qb], do_s[h, qb]
        lse, delta = lse_s[h, qb], delta_s[h, qb]

        def step(kb, dqt, diagonal=False):
            pr = jnp.exp(scores(h, qb, kb, diagonal) - lse)
            dp = dot(v_s[h, kb], do, NT)
            ds = (pr * (dp - delta)).astype(BF16)
            dv_s[kb] += dot(pr.astype(BF16), do, NN)
            dk_s[kb] += dot(ds, q, NN)
            return dqt + dot(kt_s[h, kb], ds, NN)
        dqt = lax.fori_loop(0, qb, step, jnp.zeros((HD, t_rows), F32))
        dqt = step(qb, dqt, True) * (HD ** -0.5)
        gproj[p, qb, :, e * HD:(e + 1) * HD] = dqt.T.astype(BF16)

    def pair_back(p):
        for e in range(2):
            h = 2 * p + e
            dk_s[...] = jnp.zeros_like(dk_s)
            dv_s[...] = jnp.zeros_like(dv_s)

            def one(qb, _):
                attend_back(h, e, p, qb)
                return 0
            lax.fori_loop(0, n, one, 0)
            for b in range(n):
                gproj[p, b, :, pw + e * HD:pw + (e + 1) * HD] = dk_s[b].astype(BF16)
                gproj[p, b, :, 2 * pw + e * HD:2 * pw + (e + 1) * HD] = dv_s[b].astype(BF16)

        def grad_qkv(i, _):
            a = whole(n1, pl.ds(pl.multiple_of(i * hc, hc), hc))
            gwq[p, i] = dot(a, gproj[p].reshape(n * t_rows, 3 * pw), TN).astype(BF16).reshape(nf, rows, 3 * pw)
            return 0
        lax.fori_loop(0, n, grad_qkv, 0)

    pair_back(1 - r)
    g_y(QKV)
    g_f(BACK)
    g_z(OUT)
    pair_back(r)
    rs_sent(1)
    for d in (3, 2, 1, 0):
        for h in range(2):
            gp = jnp.concatenate([gproj[p, rel(d)] for p in range(2)], 1)
            wide = jnp.concatenate([wq[p, pl.ds(h * (n // 2), n // 2)].reshape(half_w, 3 * pw) for p in range(2)], 1)
            rs_put(3, d, h, dot(gp, wide, NT))
    g_z(QKV)
    g_f(IN)
    g_f(OUT)
    rs_arrived(3)

    def ln1_back(rw, accs):
        gain, shift = accs
        g = rs_rows(3, rw)
        z, rstd = norm_parts(tok[rw].astype(F32))
        gx_o[rw] = gres[rw] + norm_back(g, z, rstd, vec(0))
        return gain + fold(g * z), shift + fold(g)
    accs = chunks(ln1_back, (zero8, zero8), 16)
    sums[0], sums[1] = accs[0], accs[1]

    for i in range(8):
        row = jnp.sum(sums[i], 0, keepdims=True) if i < 6 else jnp.zeros((1, width), F32)
        for c2 in range(n):
            v6[c2, i:i + 1, :] = row[:, c2 * hc:(c2 + 1) * hc]
    for d in (1, 2, 3):
        send(v6.at[rel(d)], v6r.at[c], vc_s.at[d], vc_r.at[c], on_ctx(d))
    vs[...] = jnp.zeros_like(vs)
    for p in range(2):
        gsum = jnp.sum(gproj[p].reshape(n * t_rows, 3 * pw).astype(F32), 0, keepdims=True)
        v6[c, 6:7, p * pw:(p + 1) * pw] = gsum[:, :pw]
        v6[c, 7:8, p * pw:(p + 1) * pw] = gsum[:, 2 * pw:]
    for j in range(2):
        row = jnp.sum(ibg[j], 0, keepdims=True)
        for k in range(2):
            i = 8 + 2 * j + k
            vs[i:i + 1, :] = row[:, k * hc:(k + 1) * hc]
    for d in (1, 2, 3):
        arrived(v6r.at[rel(d)], vc_r.at[rel(d)], on_ctx(d))
    vs[0:8] = v6[c] + v6r[rel(1)] + v6r[rel(2)] + v6r[rel(3)]
    send(vs, vy, vy_s.at[0], vy_r.at[0], on_y)
    g_e(IN)
    g_f(QKV)
    arrived(vy, vy_r.at[0], on_y)
    vs2[...] = vs[...] + vy[...]
    for s in range(1, nf):
        send(vs2, vz.at[f], vz_s.at[s], vz_r.at[f], on_z((f + s) % nf))
    g_e(QKV)
    g_out(BACK)
    g_out(OUT)
    g_out(IN)
    tot = vs2[...]
    for s in range(1, nf):
        f2 = (f + s) % nf
        arrived(vz.at[f2], vz_r.at[f2], on_z(f2))
        tot = tot + vz[f2]
    gv_o[...] = tot
    g_out(QKV)
    rs_sent(2)
    rs_sent(3)
    for end in ends:
        end()


def shards(n, nf, tokens, segments, ln1_gain, ln1_bias, w_qkv, q_bias, v_bias, w_out, out_bias,
           ln2_gain, ln2_bias, w_in, in_bias, w_back, back_bias, cotangent):
    t_rows, width = tokens.shape[1], tokens.shape[2]
    rows, brows = w_qkv.shape[0], w_back.shape[0]
    ffc = w_in.shape[1] // n
    slots = segments.shape[1]
    heads = H // n
    hc, half_w, half_f = width // n, width // 2, ffc // 2
    q3 = 3 * hc // 2
    small = jnp.stack([ln1_gain, ln1_bias, q_bias, v_bias, out_bias, ln2_gain, ln2_bias, back_bias])
    small = jnp.concatenate([small, in_bias.reshape(4, rows), jnp.zeros((4, rows), BF16)], 0)
    small = jnp.pad(small, ((0, 0), (0, 128 - rows)))
    dims = (n, nf, t_rows, width, rows, brows, ffc)
    vm = pltpu.VMEM
    dma = pltpu.SemaphoreType.DMA
    per_head = (heads, n, t_rows, HD)
    per_head_t = (heads, n, HD, t_rows)
    scratch = [
        vm((2, n, nf, rows, q3), BF16), vm((2, nf, rows, half_w), BF16), vm((2, n, nf, rows, half_f), BF16),
        vm((2, nf, brows, half_w), BF16), vm((n, nf, 16, 128), BF16), vm((width // 128, 8, 128), F32), vm((8, ffc), F32),
        vm((n, t_rows, width), BF16), vm((n, t_rows, width), BF16), vm((n, t_rows, width), BF16), vm((n, t_rows, width), BF16),
        vm(per_head, BF16), vm(per_head, BF16), vm(per_head, BF16), vm(per_head, BF16), vm(per_head_t, BF16), vm(per_head_t, BF16),
        vm((n, heads, HD, t_rows), BF16), vm((n, t_rows, ffc), BF16), vm((n, t_rows, ffc), BF16), vm((2, n, t_rows, q3), BF16),
        vm((n, 1, t_rows), jnp.int32), vm((heads, n, 1, t_rows), F32), vm((heads, n, 1, t_rows), F32),
        vm((t_rows, width), F32), vm((t_rows, width), F32), vm((t_rows, width), F32), vm((t_rows, half_f), F32), vm((t_rows, half_f), F32),
        vm((2, 3, 2, t_rows, half_w), BF16), vm((4, 3, 2, t_rows, half_w), BF16),
        vm((n, t_rows, HD), F32), vm((n, t_rows, HD), F32),
        vm((2, n, nf, rows, q3), BF16), vm((2, nf, rows, half_w), BF16), vm((2, n, nf, rows, half_f), BF16), vm((2, nf, brows, half_w), BF16),
        vm((n, nf, rows, q3), BF16), vm((nf, rows, half_w), BF16), vm((n, nf, rows, half_f), BF16), vm((nf, brows, half_w), BF16),
        vm((nf, n, rows, q3), BF16), vm((nf, rows, half_w), BF16), vm((nf, n, rows, half_f), BF16), vm((nf, brows, half_w), BF16),
        vm((n, rows, q3), BF16), vm((n, rows, half_f), BF16),
        vm((2, n, rows, q3), BF16), vm((2, rows, half_w), BF16), vm((2, n, rows, half_f), BF16), vm((2, brows, half_w), BF16),
        vm((n, 8, hc), F32), vm((n, 8, hc), F32), vm((16, hc), F32), vm((16, hc), F32), vm((16, hc), F32), vm((nf, 16, hc), F32),
        vm((2, 8, half_f), F32), vm((8, 8, width), F32),
        dma((5,)), dma((4,)), dma((n,)), dma((nf,)), dma((nf,)), dma((2, 4)), dma((2, n)),
        dma((4, 2, nf)), dma((4, nf)), dma((4, nf)), dma((4, nf)), dma((4, 3)), dma((4, n)), dma((4, 3, 2)), dma((4, 3, 2)),
        dma((4,)), dma((4,)), dma((4, nf)), dma((4, nf)), dma((2, 4)), dma((2, n)), dma((4,)), dma((4,)),
        dma((4,)), dma((n,)), dma((1,)), dma((1,)), dma((nf,)), dma((nf,)),
    ]
    shape = jax.ShapeDtypeStruct
    in_vmem, in_hbm = pl.BlockSpec(memory_space=vm), pl.BlockSpec(memory_space=pl.ANY)
    outs = pl.pallas_call(
        functools.partial(body, dims),
        out_shape=[shape((t_rows, width), BF16), shape((t_rows, width), F32), shape(w_qkv.shape, F32), shape(w_out.shape, F32),
                   shape(w_in.shape, F32), shape(w_back.shape, F32), shape((16, hc), F32)],
        in_specs=[in_vmem, in_hbm, in_vmem, in_vmem] + [in_hbm] * 4,
        out_specs=[in_vmem] * 7,
        scratch_shapes=scratch,
        compiler_params=pltpu.CompilerParams(collective_id=0, has_side_effects=True, vmem_limit_bytes=67043328),
    )(tokens[0], cotangent[0], segments, small, w_qkv, w_out, w_in, w_back)
    layer_output, input_grad, g_qkv, g_out, g_in, g_back, gv = outs
    f = lax.axis_index("fsdp")
    mine = lax.dynamic_slice_in_dim(gv[:8], f * rows, rows, 1)
    g_in_bias = lax.dynamic_slice_in_dim(gv[8:12].reshape(-1), f * 4 * rows, 4 * rows, 0)
    return (layer_output[None], input_grad[None], mine[0], mine[1], g_qkv, mine[6], mine[7], g_out,
            mine[2], mine[3], mine[4], g_in, g_in_bias, g_back, mine[5])


def solution(mesh):
    both = ("ctx", "fsdp")
    own, rows = P(both), P(both, None)
    seqs = P(("fsdp", "rep"), "ctx", None)
    in_specs = (seqs, P(("fsdp", "rep"), None), own, own, rows, own, own, rows, own, own, own, rows, own, rows, own, seqs)
    out_specs = (seqs, seqs, own, own, rows, own, own, rows, own, own, own, rows, own, rows, own)
    run = functools.partial(shards, mesh.shape["ctx"], mesh.shape["fsdp"])
    return jax.shard_map(run, mesh=mesh, in_specs=in_specs, out_specs=out_specs, check_vma=False)
```

```python
import functools

import jax
import jax.numpy as jnp
from jax import lax
from jax.experimental import pallas as pl
from jax.experimental.pallas import tpu as pltpu
from jax.sharding import PartitionSpec as P

H = 16
HD = 64
DOCS = 5
EPS = 1e-05
MASKED = -1e30
F32, BF16 = jnp.float32, jnp.bfloat16
MESH = pl.DeviceIdType.MESH
NN = ((1,), (0,))
NT = ((1,), (1,))
TN = ((0,), (0,))
QKV, OUT, IN, BACK = range(4)
CHUNK = 32


def dot(a, b, dims):
    return lax.dot_general(a, b, (dims, ((), ())), preferred_element_type=F32)


def norm_parts(x):
    center = x - jnp.mean(x, -1, keepdims=True)
    rstd = lax.rsqrt(jnp.mean(center * center, -1, keepdims=True) + EPS)
    return center * rstd, rstd


def norm_back(g, z, rstd, gain):
    gz = g * gain
    return rstd * (gz - jnp.mean(gz, -1, keepdims=True) - z * jnp.mean(gz * z, -1, keepdims=True))


def gelu_both(t):
    a, b = 0.7978845608028654, 0.044715
    t2 = t * t
    th = jnp.tanh(a * t * (1.0 + b * t2))
    half = 0.5 * (1.0 + th)
    return t * half, half + 0.5 * t * (1.0 - th * th) * (a * (1.0 + 3.0 * b * t2))


def fold(x):
    return jnp.sum(x.reshape(x.shape[0] // 8, 8, x.shape[1]), 0)


def body(dims, tok, cot_in, seg, pack, wq_hbm, wo_hbm, wi_hbm, wb_hbm,
         out_o, gx_o, gq_o, go_o, gi_o, gb_o, gv_o,
         wq, wo, wi, wb, packs, vecs, inb, n1, cot, n2, gbr, q_s, k_s, v_s, do_s, kt_s, vt_s, att, act, gpre, gproj,
         start_s, lse_s, delta_s, resid, gres, keep, tmp1, tmp2, snd, land,
         dk_s, dv_s, gwq, gwo, gwi, gwb, yq, yo, yi, yb, zq, zo, zi, zb, fq, fi, aq, ao, ai, ab,
         v6, v6r, vs, vy, vs2, vz, ibg, sums,
         loc, pk_cs, pk_cr, pk_zs, pk_zr, wc_s, wc_r, wz_s, wz_r, wy_s, wy_r, ag_s, ag_r, rs_s, rs_r,
         gy_s, gy_r, gz_s, gz_r, gc_s, gc_r, gf_s, gf_r, vc_s, vc_r, vy_s, vy_r, vz_s, vz_r, out_s):
    n, nf, t_rows, width, rows, brows, ffc = dims
    half_w, half_f = width // 2, ffc // 2
    hc = width // n
    pw = hc // 2
    c, f, r = lax.axis_index("ctx"), lax.axis_index("fsdp"), lax.axis_index("rep")
    x, core = c // 2, c % 2

    def rel(d):
        return ((x + d // 2) % 2) * 2 + (core + d % 2) % 2

    def on_ctx(d):
        return (rel(d), f, r)

    def on_z(f2):
        return (c, f2, r)

    on_y = (c, f, 1 - r)
    ends = []

    def make(src, dst, ss, rs, dev):
        return pltpu.make_async_remote_copy(src_ref=src, dst_ref=dst, send_sem=ss, recv_sem=rs, device_id=dev,
                                            device_id_type=MESH)

    def send(src, dst, ss, rs, dev, cond=None):
        if cond is None:
            make(src, dst, ss, rs, dev).start()
            ends.append(lambda: make(src, dst, ss, rs, dev).wait_send())
        else:
            @pl.when(cond)
            def _():
                make(src, dst, ss, rs, dev).start()

            def end():
                @pl.when(cond)
                def _():
                    make(src, dst, ss, rs, dev).wait_send()
            ends.append(end)

    def arrived(dst, rs, dev):
        make(dst, dst, rs, rs, dev).wait_recv()

    def local(src, dst, sem):
        pltpu.make_async_copy(src, dst, sem).start()

    def local_done(dst, sem):
        pltpu.make_async_copy(dst, dst, sem).wait()

    for h in range(2):
        for j in range(3):
            local(wq_hbm.at[:, pl.ds(pl.multiple_of(j * width + c * hc + h * pw, pw), pw)],
                  wq.at[h, c, f, :, pl.ds(j * pw, pw)], loc.at[1])
        local(wo_hbm.at[:, pl.ds(h * half_w, half_w)], wo.at[h, f], loc.at[2])
        local(wb_hbm.at[:, pl.ds(h * half_w, half_w)], wb.at[h, f], loc.at[4])
    for h in range(2):
        local(wi_hbm.at[:, pl.ds(pl.multiple_of(c * ffc + h * half_f, half_f), half_f)], wi.at[h, c, f], loc.at[3])
    local(cot_in, cot.at[c], loc.at[0])
    packs[c, f] = pack[...]
    barrier = pltpu.get_barrier_semaphore()
    peers = [on_ctx(d) for d in (1, 2, 3)] + [on_z((f + s) % nf) for s in range(1, nf)] + [on_y]
    for dev in peers:
        pl.semaphore_signal(barrier, inc=1, device_id=dev, device_id_type=MESH)
    pl.semaphore_wait(barrier, len(peers))

    for d in (1, 2, 3):
        send(packs.at[c, f], packs.at[c, f], pk_cs.at[d], pk_cr.at[c], on_ctx(d))

    def exchange(kind, hbm, buf, parts, step, w):
        for d in (2, 3, 1):
            c2 = rel(d)
            for h in range(2):
                for j in range(parts):
                    make(hbm.at[:, pl.ds(pl.multiple_of(j * width + c2 * step + h * w, w), w)],
                         buf.at[h, c, f, :, pl.ds(j * w, w)], wc_s.at[kind, d], wc_r.at[kind, c], on_ctx(d)).start()
            ends.append(lambda d=d: make(buf.at[:, c, f], buf.at[:, c, f], wc_s.at[kind, d], wc_r.at[kind, c],
                                         on_ctx(d)).wait_send())

    def exchanged(kind, buf):
        for d in (1, 2, 3):
            arrived(buf.at[:, rel(d), f], wc_r.at[kind, rel(d)], on_ctx(d))

    exchange(0, wq_hbm, wq, 3, hc, pw)
    exchange(1, wi_hbm, wi, 1, ffc, half_f)

    bufs = {QKV: wq, OUT: wo, IN: wi, BACK: wb}

    def block(buf, kind, h, f2):
        return buf.at[h, :, f2] if kind in (QKV, IN) else buf.at[h, f2]

    pieces = {QKV: 2, OUT: 1, IN: 2, BACK: 2}

    def part(kind, h, f2, p):
        buf = bufs[kind]
        if kind in (QKV, IN):
            return buf.at[h, pl.ds(p * (n // 2), n // 2), f2]
        return buf.at[h, f2] if kind == OUT else buf.at[h, f2, pl.ds(p * (brows // 2), brows // 2)]

    def w_z(kind, p, slot, src, dst, cond):
        b = part(kind, r, src, p)
        send(b, b, wz_s.at[kind, p, slot], wz_r.at[kind, p, src], on_z(dst), cond)

    def w_own(kind, p):
        for k, s in enumerate([1] + list(range(3, nf))):
            w_z(kind, p, 2 + 2 * k, f, f + s, f + s < nf)
            w_z(kind, p, 3 + 2 * k, f, f - s, f >= s)

    def sources(s):
        return (f - s, f >= s), (f + s, f + s < nf)

    def w_relay(kind, p):
        for way, (src, ok) in enumerate(sources(1)):
            w_z(kind, p, way, src, 2 * f - src, ok & ((f + 1 < nf) if way == 0 else (f >= 1)))

    def w_swap(kind, p, s):
        for src, ok in sources(s):
            b = part(kind, r, src, p)

            @pl.when(ok)
            def _():
                arrived(b, wz_r.at[kind, p, src], on_y)
            send(b, b, wy_s.at[kind, p, src], wy_r.at[kind, p, src], on_y, ok)

    def w_step(kind, p, s):
        if s == 3:
            for far in range(3, nf):
                w_swap(kind, p, far)
        elif s < nf:
            w_swap(kind, p, s)
            if s == 1:
                w_relay(kind, p)

    def w_arrived(kind):
        for p in range(pieces[kind]):
            for s in range(1, nf):
                f2 = (f + s) % nf
                arrived(part(kind, 1 - r, f2, p), wy_r.at[kind, p, f2], on_y)

    def ag_start(i, buf):
        for d, k in ((2, 0), (1, 1)):
            send(buf.at[c], buf.at[c], ag_s.at[i, k], ag_r.at[i, c], on_ctx(d))

    def ag_forward(i, buf):
        b = rel(2)
        arrived(buf.at[b], ag_r.at[i, b], on_ctx(2))
        send(buf.at[b], buf.at[b], ag_s.at[i, 2], ag_r.at[i, b], on_ctx(1))

    def ag_wait(i, buf, d):
        arrived(buf.at[rel(d)], ag_r.at[i, rel(d)], on_ctx(d))

    def rs_put(i, d, h, val):
        cols = pl.ds(h * half_w, half_w)
        if d == 0:
            keep[:, cols] = val
            return
        k = {3: 0, 2: 1, 1: 2}[d]
        if d == 2:
            arrived(land.at[i, 0, h], rs_r.at[i, 0, h], on_ctx(1))
            val = val + land[i, 0, h].astype(F32)
        snd[i % 2, k, h] = val.astype(BF16)
        make(snd.at[i % 2, k, h], land.at[i, k, h], rs_s.at[i, k, h], rs_r.at[i, k, h], on_ctx(2 if d == 2 else 1)).start()

    def rs_sent(i):
        for d, k in ((3, 0), (2, 1), (1, 2)):
            for h in range(2):
                make(snd.at[i % 2, k, h], land.at[i, k, h], rs_s.at[i, k, h], rs_r.at[i, k, h],
                     on_ctx(2 if d == 2 else 1)).wait_send()

    def rs_arrived(i):
        for h in range(2):
            arrived(land.at[i, 2, h], rs_r.at[i, 2, h], on_ctx(1))
            arrived(land.at[i, 1, h], rs_r.at[i, 1, h], on_ctx(2))

    def rs_rows(i, rw):
        parts = [keep[rw, pl.ds(h * half_w, half_w)] + land[i, 1, h, rw].astype(F32) + land[i, 2, h, rw].astype(F32)
                 for h in range(2)]
        return jnp.concatenate(parts, 1)

    def chunks(fn, init=0, size=CHUNK):
        return lax.fori_loop(0, t_rows // size, lambda i, v: fn(pl.ds(pl.multiple_of(i * size, size), size), v), init)

    sg = seg[...]
    start = jnp.zeros_like(sg)
    for doc in range(DOCS - 1):
        start = start + jnp.where(sg > doc, jnp.sum((sg == doc).astype(jnp.int32), -1, keepdims=True), 0)
    for b in range(n):
        start_s[b] = start[:, b * t_rows:(b + 1) * t_rows]

    local_done(wo.at[:, f], loc.at[2])
    w_own(OUT, 0)
    local_done(wb.at[:, f], loc.at[4])
    w_own(BACK, 0)
    for d in (1, 2, 3):
        arrived(packs.at[rel(d), f], pk_cr.at[rel(d)], on_ctx(d))
    for s in range(1, nf):
        f2 = (f + s) % nf
        send(packs.at[:, f], packs.at[:, f], pk_zs.at[s], pk_zr.at[f], on_z(f2))
    local_done(wq.at[:, c, f], loc.at[1])
    exchanged(0, wq)
    w_own(QKV, 0)
    w_own(QKV, 1)
    w_swap(OUT, 0, 1)
    w_swap(BACK, 0, 1)
    for s in range(1, nf):
        f2 = (f + s) % nf
        arrived(packs.at[:, f2], pk_zr.at[f2], on_z(f2))
    lane = lax.broadcasted_iota(jnp.int32, (8, 128), 1)
    per = 128 // rows
    for g in range(width // 128):
        acc = None
        for j in range(per):
            e = g * per + j
            piece = packs[e // nf, e % nf].astype(F32)[0:8]
            acc = piece if j == 0 else jnp.where(lane // rows == j, pltpu.roll(piece, j * rows, 1), acc)
        vecs[g] = acc
    for g in range(ffc // 128):
        acc = None
        for j in range(per):
            e = g * per + j
            k = e % 4
            piece = packs[c, e // 4].astype(F32)[8:16]
            piece = jnp.broadcast_to(piece[k:k + 1], (8, 128))
            acc = piece if j == 0 else jnp.where(lane // rows == j, pltpu.roll(piece, j * rows, 1), acc)
        inb[:, g * 128:(g + 1) * 128] = acc

    def vec(v):
        return jnp.concatenate([vecs[g, v:v + 1, :] for g in range(width // 128)], 1)

    def ln1(rw, _):
        z, _r = norm_parts(tok[rw].astype(F32))
        n1[c, rw] = (z * vec(0) + vec(1)).astype(BF16)
        return 0
    chunks(ln1)
    ag_start(0, n1)
    local_done(cot.at[c], loc.at[0])
    ag_start(1, cot)
    w_step(QKV, 0, 1)
    w_step(QKV, 1, 1)
    w_relay(OUT, 0)
    local_done(wi.at[:, c, f], loc.at[3])
    exchanged(1, wi)
    w_own(IN, 0)
    w_own(IN, 1)
    w_relay(BACK, 0)
    w_own(BACK, 1)
    for s in (3, 2):
        w_step(QKV, 0, s)
        w_step(QKV, 1, s)
    w_step(OUT, 0, 3)
    w_step(OUT, 0, 2)
    ag_forward(0, n1)
    ag_wait(0, n1, 1)
    ag_wait(0, n1, 3)
    w_arrived(QKV)

    def project(b, _):
        for p in range(2):
            pr = dot(n1[b], wq[p].reshape(width, 3 * pw), NN)
            qv = ((pr[:, :pw] + vecs[c * 2 + p, 2:3, :]).astype(BF16).astype(F32) * (HD ** -0.5)).astype(BF16)
            kv = pr[:, pw:2 * pw].astype(BF16)
            vv = (pr[:, 2 * pw:] + vecs[c * 2 + p, 3:4, :]).astype(BF16)
            kt, vt = kv.T, vv.T
            for e in range(2):
                q_s[2 * p + e, b] = qv[:, e * HD:(e + 1) * HD]
                k_s[2 * p + e, b] = kv[:, e * HD:(e + 1) * HD]
                v_s[2 * p + e, b] = vv[:, e * HD:(e + 1) * HD]
                kt_s[2 * p + e, b] = kt[e * HD:(e + 1) * HD]
                vt_s[2 * p + e, b] = vt[e * HD:(e + 1) * HD]
        return 0
    lax.fori_loop(0, n, project, 0)

    key_row = lax.broadcasted_iota(jnp.int32, (t_rows, t_rows), 0)
    query_col = lax.broadcasted_iota(jnp.int32, (t_rows, t_rows), 1)

    def scores(h, qb, kb, diagonal):
        s = dot(k_s[h, kb], q_s[h, qb], NT)
        ok = key_row >= start_s[qb] - kb * t_rows
        if diagonal:
            ok = ok & (key_row <= query_col)
        return jnp.where(ok, s, MASKED)

    def attend(h, qb):
        def step(kb, carry, diagonal=False):
            m, l, acc = carry
            s = scores(h, qb, kb, diagonal)
            m2 = jnp.maximum(m, jnp.max(s, 0, keepdims=True))
            p = jnp.exp(s - m2)
            a = jnp.exp(m - m2)
            return m2, l * a + jnp.sum(p, 0, keepdims=True), acc * a + dot(vt_s[h, kb], p.astype(BF16), NN)
        zero = jnp.zeros((1, t_rows), F32)
        carry = lax.fori_loop(0, qb, step, (zero + MASKED, zero, jnp.zeros((HD, t_rows), F32)))
        m, l, acc = step(qb, carry, True)
        att[qb, h] = (acc / l).astype(BF16)
        lse_s[h, qb] = m + jnp.log(l)

    polls = [[(IN, 0, 1), (IN, 0, 3)], [(BACK, 0, 3), (BACK, 0, 2)], [(IN, 1, 1), (IN, 1, 3)], [], [(BACK, 1, 1)], [(BACK, 1, 3)],
             [(IN, 0, 2)], [(IN, 1, 2)]]
    for d in (3, 2, 1, 0):
        qb = rel(d)
        for k in range(2):
            def heads(h, _):
                attend(h, qb)
                return 0
            lax.fori_loop(k * (H // n // 2), (k + 1) * (H // n // 2), heads, 0)
            for poll in polls[2 * (3 - d) + k]:
                w_step(*poll)
        if d == 3:
            w_arrived(OUT)
        if d == 2:
            ag_forward(1, cot)
        for h in range(2):
            rs_put(0, d, h, dot(att[qb].reshape(hc, t_rows), wo[h].reshape(hc, half_w), TN))
    rs_arrived(0)

    def ln2(rw, _):
        res = tok[rw].astype(F32) + rs_rows(0, rw) + vec(4)
        resid[rw] = res
        z, _r = norm_parts(res)
        n2[c, rw] = (z * vec(5) + vec(6)).astype(BF16)
        return 0
    chunks(ln2)
    ag_start(2, n2)
    w_step(BACK, 1, 2)
    w_arrived(IN)
    ag_wait(1, cot, 1)
    ag_wait(1, cot, 3)
    w_arrived(BACK)

    ibg[...] = jnp.zeros_like(ibg)
    for d in (0, 1, 3, 2):
        b = rel(d)
        if d == 1:
            ag_wait(2, n2, 1)
        if d == 3:
            ag_forward(2, n2)
            ag_wait(2, n2, 3)

        def up(j, _):
            tmp1[...] = dot(n2[b], wi[j].reshape(width, half_f), NN)
            wide = jnp.concatenate([wb[h, pl.ds(j * (nf // 2), nf // 2)].reshape(half_f, half_w) for h in range(2)], 1)
            tmp2[...] = dot(cot[b], wide, NT)
            bias = inb[0:1, pl.ds(pl.multiple_of(j * half_f, half_f), half_f)]
            cols = pl.ds(pl.multiple_of(j * half_f, half_f), half_f)

            def one(rw, acc):
                a, da = gelu_both(tmp1[rw] + bias)
                act[b, rw, cols] = a.astype(BF16)
                gp = (tmp2[rw] * da).astype(BF16)
                gpre[b, rw, cols] = gp
                return acc + fold(gp.astype(F32))
            ibg[j] += chunks(one, jnp.zeros((8, half_f), F32))
            return 0
        lax.fori_loop(0, 2, up, 0)
        if d == 3:
            rs_sent(0)
        for h in range(2):
            wide = jnp.concatenate([wi[j, pl.ds(h * (n // 2), n // 2)].reshape(half_w, half_f) for j in range(2)], 1)
            rs_put(1, d, h, dot(gpre[b], wide, NT))

    grads = {QKV: (gwq, yq, zq), OUT: (gwo, yo, zo), IN: (gwi, yi, zi), BACK: (gwb, yb, zb)}
    alls = {QKV: aq, OUT: ao, IN: ai, BACK: ab}

    def g_y(kind):
        g, y, _z = grads[kind]
        send(g.at[1 - r], y, gy_s.at[kind], gy_r.at[kind], on_y)

    def g_z(kind):
        g, y, z = grads[kind]
        arrived(y, gy_r.at[kind], on_y)

        def add(i, _):
            g[r, i] = (g[r, i].astype(F32) + y[i].astype(F32)).astype(BF16)
            return 0
        lax.fori_loop(0, y.shape[0], add, 0)
        for s in range(1, nf):
            f2 = (f + s) % nf
            send(block(g, kind, r, f2), z.at[f], gz_s.at[kind, s], gz_r.at[kind, f], on_z(f2))

    def g_f(kind):
        g, _y, z = grads[kind]
        for s in range(1, nf):
            f2 = (f + s) % nf
            arrived(z.at[f2], gz_r.at[kind, f2], on_z(f2))
        if kind in (QKV, IN):
            fin, k = (fq, 0) if kind == QKV else (fi, 1)

            def add(i, _):
                tot = g[r, i, f].astype(F32)
                for s in range(1, nf):
                    tot = tot + z[(f + s) % nf, i].astype(F32)
                fin[i] = tot.astype(BF16)
                return 0
            lax.fori_loop(0, n, add, 0)
            for d in (2, 3, 1):
                send(fin.at[rel(d)], alls[kind].at[r, c], gc_s.at[k, d], gc_r.at[k, c], on_ctx(d))
            alls[kind][r, c] = fin[c]
        else:
            tot = g[r, f].astype(F32)
            for s in range(1, nf):
                tot = tot + z[(f + s) % nf].astype(F32)
            alls[kind][r] = tot.astype(BF16)
            send(alls[kind].at[r], alls[kind].at[r], gf_s.at[kind], gf_r.at[kind], on_y)

    def g_e(kind):
        k = 0 if kind == QKV else 1
        a = alls[kind]
        for d in (1, 2, 3):
            arrived(a.at[r, rel(d)], gc_r.at[k, rel(d)], on_ctx(d))
        send(a.at[r], a.at[r], gf_s.at[kind], gf_r.at[kind], on_y)

    outs = {QKV: gq_o, OUT: go_o, IN: gi_o, BACK: gb_o}

    def g_out(kind):
        a, o = alls[kind], outs[kind]
        arrived(a.at[1 - r], gf_r.at[kind], on_y)
        for h in range(2):
            if kind in (OUT, BACK):
                local(a.at[h], o.at[:, pl.ds(h * half_w, half_w)], out_s.at[kind])
                continue
            for c2 in range(n):
                for j in range(3 if kind == QKV else 1):
                    w = pw if kind == QKV else half_f
                    lo = j * width + c2 * hc + h * pw if kind == QKV else c2 * ffc + h * half_f
                    local(a.at[h, c2, :, pl.ds(j * w, w)], o.at[:, pl.ds(lo, w)], out_s.at[kind])

    def whole(buf, cols):
        v = buf[:, :, cols]
        return v.reshape(n * t_rows, v.shape[2])

    def grad_back(h):
        per_f = ffc // nf
        tiles = max(1, 256 // per_f)

        def one(i, _):
            a = whole(act, pl.ds(pl.multiple_of(i * 256, 256), 256))
            g = whole(cot, pl.ds(pl.multiple_of(h * half_w, half_w), half_w))
            v = dot(a, g, TN).astype(BF16)
            gwb[h, pl.ds(i * tiles, tiles)] = v.reshape(tiles, per_f, half_w)
            return 0
        lax.fori_loop(0, ffc // 256, one, 0)

    def grad_in(h):
        def one(i, _):
            a = whole(n2, pl.ds(pl.multiple_of(i * hc, hc), hc))
            g = whole(gpre, pl.ds(pl.multiple_of(h * half_f, half_f), half_f))
            gwi[h, i] = dot(a, g, TN).astype(BF16).reshape(nf, rows, half_f)
            return 0
        lax.fori_loop(0, n, one, 0)

    grad_back(1 - r)
    g_y(BACK)
    grad_back(r)
    rs_arrived(1)

    def ln2_back(rw, accs):
        gain, shift, bb, ob = accs
        g = rs_rows(1, rw)
        z, rstd = norm_parts(resid[rw])
        ct = cot[c, rw].astype(F32)
        gr = ct + norm_back(g, z, rstd, vec(5))
        gres[rw] = gr
        low = gr.astype(BF16)
        gbr[c, rw] = low
        return gain + fold(g * z), shift + fold(g), bb + fold(ct), ob + fold(low.astype(F32))
    zero8 = jnp.zeros((8, width), F32)
    accs = chunks(ln2_back, (zero8, zero8, zero8, zero8), 16)
    for i, a in zip((3, 4, 5, 2), accs):
        sums[i] = a
    ag_start(3, gbr)
    grad_in(1 - r)
    g_y(IN)
    grad_in(r)
    g_z(BACK)
    ag_forward(3, gbr)

    for d in (3, 2, 1, 0):
        for h in range(2):
            rs_put(2, d, h, dot(act[rel(d)], wb[h].reshape(ffc, half_w), NN))
    ag_wait(3, gbr, 1)
    ag_wait(3, gbr, 3)

    def g_attended(b, _):
        wide = jnp.concatenate([wo[h].reshape(hc, half_w) for h in range(2)], 1)
        g = dot(gbr[b], wide, NT).astype(BF16)
        gt = g.T.astype(F32).reshape(H // n, HD, t_rows)
        for h in range(H // n):
            do_s[h, b] = g[:, h * HD:(h + 1) * HD]
            delta_s[h, b] = jnp.sum(gt[h] * att[b, h].astype(F32), 0, keepdims=True)
        return 0
    lax.fori_loop(0, n, g_attended, 0)
    g_z(IN)

    def grad_out(h):
        tot = jnp.zeros((hc, half_w), F32)
        cols = pl.ds(pl.multiple_of(h * half_w, half_w), half_w)
        for b in range(n):
            tot = tot + dot(att[b].reshape(hc, t_rows), gbr[b, :, cols], NN)
        gwo[h] = tot.astype(BF16).reshape(nf, rows, half_w)
    grad_out(1 - r)
    g_y(OUT)
    grad_out(r)

    rs_arrived(2)

    def finish_out(rw, _):
        out_o[rw] = (resid[rw] + rs_rows(2, rw) + vec(7)).astype(BF16)
        return 0
    chunks(finish_out)

    def attend_back(h, e, p, qb):
        q, do = q_s[h, qb], do_s[h, qb]
        lse, delta = lse_s[h, qb], delta_s[h, qb]

        def step(kb, dqt, diagonal=False):
            pr = jnp.exp(scores(h, qb, kb, diagonal) - lse)
            dp = dot(v_s[h, kb], do, NT)
            ds = (pr * (dp - delta)).astype(BF16)
            dv_s[kb] += dot(pr.astype(BF16), do, NN)
            dk_s[kb] += dot(ds, q, NN)
            return dqt + dot(kt_s[h, kb], ds, NN)
        dqt = lax.fori_loop(0, qb, step, jnp.zeros((HD, t_rows), F32))
        dqt = step(qb, dqt, True) * (HD ** -0.5)
        gproj[p, qb, :, e * HD:(e + 1) * HD] = dqt.T.astype(BF16)

    def pair_back(p):
        for e in range(2):
            h = 2 * p + e
            dk_s[...] = jnp.zeros_like(dk_s)
            dv_s[...] = jnp.zeros_like(dv_s)

            def one(qb, _):
                attend_back(h, e, p, qb)
                return 0
            lax.fori_loop(0, n, one, 0)
            for b in range(n):
                gproj[p, b, :, pw + e * HD:pw + (e + 1) * HD] = dk_s[b].astype(BF16)
                gproj[p, b, :, 2 * pw + e * HD:2 * pw + (e + 1) * HD] = dv_s[b].astype(BF16)

        def grad_qkv(i, _):
            a = whole(n1, pl.ds(pl.multiple_of(i * hc, hc), hc))
            gwq[p, i] = dot(a, gproj[p].reshape(n * t_rows, 3 * pw), TN).astype(BF16).reshape(nf, rows, 3 * pw)
            return 0
        lax.fori_loop(0, n, grad_qkv, 0)

    pair_back(1 - r)
    g_y(QKV)
    g_f(BACK)
    g_z(OUT)
    pair_back(r)
    rs_sent(1)
    for d in (3, 2, 1, 0):
        for h in range(2):
            gp = jnp.concatenate([gproj[p, rel(d)] for p in range(2)], 1)
            wide = jnp.concatenate([wq[p, pl.ds(h * (n // 2), n // 2)].reshape(half_w, 3 * pw) for p in range(2)], 1)
            rs_put(3, d, h, dot(gp, wide, NT))
    g_z(QKV)
    g_f(IN)
    g_f(OUT)
    rs_arrived(3)

    def ln1_back(rw, accs):
        gain, shift = accs
        g = rs_rows(3, rw)
        z, rstd = norm_parts(tok[rw].astype(F32))
        gx_o[rw] = gres[rw] + norm_back(g, z, rstd, vec(0))
        return gain + fold(g * z), shift + fold(g)
    accs = chunks(ln1_back, (zero8, zero8), 16)
    sums[0], sums[1] = accs[0], accs[1]

    for i in range(8):
        row = jnp.sum(sums[i], 0, keepdims=True) if i < 6 else jnp.zeros((1, width), F32)
        for c2 in range(n):
            v6[c2, i:i + 1, :] = row[:, c2 * hc:(c2 + 1) * hc]
    for d in (1, 2, 3):
        send(v6.at[rel(d)], v6r.at[c], vc_s.at[d], vc_r.at[c], on_ctx(d))
    vs[...] = jnp.zeros_like(vs)
    for p in range(2):
        gsum = jnp.sum(gproj[p].reshape(n * t_rows, 3 * pw).astype(F32), 0, keepdims=True)
        v6[c, 6:7, p * pw:(p + 1) * pw] = gsum[:, :pw]
        v6[c, 7:8, p * pw:(p + 1) * pw] = gsum[:, 2 * pw:]
    for j in range(2):
        row = jnp.sum(ibg[j], 0, keepdims=True)
        for k in range(2):
            i = 8 + 2 * j + k
            vs[i:i + 1, :] = row[:, k * hc:(k + 1) * hc]
    for d in (1, 2, 3):
        arrived(v6r.at[rel(d)], vc_r.at[rel(d)], on_ctx(d))
    vs[0:8] = v6[c] + v6r[rel(1)] + v6r[rel(2)] + v6r[rel(3)]
    send(vs, vy, vy_s.at[0], vy_r.at[0], on_y)
    g_e(IN)
    g_f(QKV)
    arrived(vy, vy_r.at[0], on_y)
    vs2[...] = vs[...] + vy[...]
    for s in range(1, nf):
        send(vs2, vz.at[f], vz_s.at[s], vz_r.at[f], on_z((f + s) % nf))
    g_e(QKV)
    g_out(BACK)
    g_out(OUT)
    g_out(IN)
    tot = vs2[...]
    for s in range(1, nf):
        f2 = (f + s) % nf
        arrived(vz.at[f2], vz_r.at[f2], on_z(f2))
        tot = tot + vz[f2]
    mine, mine_in = tot[:, :rows], tot[8:9, :4 * rows]
    for f2 in range(1, nf):
        row, lo = 8 + f2 * 4 * rows // hc, f2 * 4 * rows % hc
        mine = jnp.where(f == f2, tot[:, f2 * rows:(f2 + 1) * rows], mine)
        mine_in = jnp.where(f == f2, tot[row:row + 1, lo:lo + 4 * rows], mine_in)
    gv_o[0:16, :rows] = mine
    gv_o[16:17, :4 * rows] = mine_in
    g_out(QKV)
    rs_sent(2)
    rs_sent(3)
    for end in ends:
        end()
    for kind in range(4):
        local_done(alls[kind], out_s.at[kind])


def finish(lo_i, gx_i, gq_i, go_i, gi_i, gb_i, lo_o, gx_o, gq_o, go_o, gi_o, gb_o,
           lo_b, gx_b, gq_b, go_b, gi_b, gb_b, gq_w, go_w, gi_w, gb_w, sem_i, sem_o):
    parts = [(gb_i, gb_b, gb_w, gb_o), (gi_i, gi_b, gi_w, gi_o), (gq_i, gq_b, gq_w, gq_o), (go_i, go_b, go_w, go_o),
             (gx_i, gx_b, gx_b, gx_o), (lo_i, lo_b, lo_b, lo_o)]
    for k, (src, low, wide, dst) in enumerate(parts):
        pltpu.make_async_copy(src, low, sem_i.at[k]).start()
    for k, (src, low, wide, dst) in enumerate(parts):
        pltpu.make_async_copy(src, low, sem_i.at[k]).wait()
        if wide is not low:
            wide[...] = low[...].astype(F32)
        pltpu.make_async_copy(wide, dst, sem_o.at[k]).start()
    for k, (src, low, wide, dst) in enumerate(parts):
        pltpu.make_async_copy(wide, dst, sem_o.at[k]).wait()


def shards(n, nf, tokens, segments, ln1_gain, ln1_bias, w_qkv, q_bias, v_bias, w_out, out_bias,
           ln2_gain, ln2_bias, w_in, in_bias, w_back, back_bias, cotangent):
    t_rows, width = tokens.shape[1], tokens.shape[2]
    rows, brows = w_qkv.shape[0], w_back.shape[0]
    ffc = w_in.shape[1] // n
    slots = segments.shape[1]
    heads = H // n
    hc, half_w, half_f = width // n, width // 2, ffc // 2
    q3 = 3 * hc // 2
    small = jnp.stack([ln1_gain, ln1_bias, q_bias, v_bias, out_bias, ln2_gain, ln2_bias, back_bias])
    small = jnp.concatenate([small, in_bias.reshape(4, rows), jnp.zeros((4, rows), BF16)], 0)
    small = jnp.pad(small, ((0, 0), (0, 128 - rows)))
    dims = (n, nf, t_rows, width, rows, brows, ffc)
    vm = pltpu.VMEM
    dma = pltpu.SemaphoreType.DMA
    per_head = (heads, n, t_rows, HD)
    per_head_t = (heads, n, HD, t_rows)
    scratch = [
        vm((2, n, nf, rows, q3), BF16), vm((2, nf, rows, half_w), BF16), vm((2, n, nf, rows, half_f), BF16),
        vm((2, nf, brows, half_w), BF16), vm((n, nf, 16, 128), BF16), vm((width // 128, 8, 128), F32), vm((8, ffc), F32),
        vm((n, t_rows, width), BF16), vm((n, t_rows, width), BF16), vm((n, t_rows, width), BF16), vm((n, t_rows, width), BF16),
        vm(per_head, BF16), vm(per_head, BF16), vm(per_head, BF16), vm(per_head, BF16), vm(per_head_t, BF16), vm(per_head_t, BF16),
        vm((n, heads, HD, t_rows), BF16), vm((n, t_rows, ffc), BF16), vm((n, t_rows, ffc), BF16), vm((2, n, t_rows, q3), BF16),
        vm((n, 1, t_rows), jnp.int32), vm((heads, n, 1, t_rows), F32), vm((heads, n, 1, t_rows), F32),
        vm((t_rows, width), F32), vm((t_rows, width), F32), vm((t_rows, width), F32), vm((t_rows, half_f), F32), vm((t_rows, half_f), F32),
        vm((2, 3, 2, t_rows, half_w), BF16), vm((4, 3, 2, t_rows, half_w), BF16),
        vm((n, t_rows, HD), F32), vm((n, t_rows, HD), F32),
        vm((2, n, nf, rows, q3), BF16), vm((2, nf, rows, half_w), BF16), vm((2, n, nf, rows, half_f), BF16), vm((2, nf, brows, half_w), BF16),
        vm((n, nf, rows, q3), BF16), vm((nf, rows, half_w), BF16), vm((n, nf, rows, half_f), BF16), vm((nf, brows, half_w), BF16),
        vm((nf, n, rows, q3), BF16), vm((nf, rows, half_w), BF16), vm((nf, n, rows, half_f), BF16), vm((nf, brows, half_w), BF16),
        vm((n, rows, q3), BF16), vm((n, rows, half_f), BF16),
        vm((2, n, rows, q3), BF16), vm((2, rows, half_w), BF16), vm((2, n, rows, half_f), BF16), vm((2, brows, half_w), BF16),
        vm((n, 8, hc), F32), vm((n, 8, hc), F32), vm((16, hc), F32), vm((16, hc), F32), vm((16, hc), F32), vm((nf, 16, hc), F32),
        vm((2, 8, half_f), F32), vm((8, 8, width), F32),
        dma((5,)), dma((4,)), dma((n,)), dma((nf,)), dma((nf,)), dma((2, 4)), dma((2, n)),
        dma((4, 2, 4 + 2 * max(0, nf - 3))), dma((4, 2, nf)), dma((4, 2, nf)), dma((4, 2, nf)), dma((4, 3)), dma((4, n)), dma((4, 3, 2)), dma((4, 3, 2)),
        dma((4,)), dma((4,)), dma((4, nf)), dma((4, nf)), dma((2, 4)), dma((2, n)), dma((4,)), dma((4,)),
        dma((4,)), dma((n,)), dma((1,)), dma((1,)), dma((nf,)), dma((nf,)), dma((4,)),
    ]
    shape = jax.ShapeDtypeStruct
    in_vmem, in_hbm = pl.BlockSpec(memory_space=vm), pl.BlockSpec(memory_space=pl.ANY)
    outs = pl.pallas_call(
        functools.partial(body, dims),
        out_shape=[shape((t_rows, width), BF16), shape((t_rows, width), F32), shape(w_qkv.shape, BF16), shape(w_out.shape, BF16),
                   shape(w_in.shape, BF16), shape(w_back.shape, BF16), shape((24, hc), F32)],
        in_specs=[in_vmem, in_hbm, in_vmem, in_vmem] + [in_hbm] * 4,
        out_specs=[in_vmem] * 2 + [in_hbm] * 4 + [in_vmem],
        scratch_shapes=scratch,
        compiler_params=pltpu.CompilerParams(collective_id=0, has_side_effects=True, vmem_limit_bytes=67043328),
    )(tokens[0], cotangent[0], segments, small, w_qkv, w_out, w_in, w_back)
    gv = outs[6]
    grads = [w_qkv, w_out, w_in, w_back]
    layer_output, input_grad, g_qkv, g_out, g_in, g_back = pl.pallas_call(
        finish,
        out_shape=[shape((t_rows, width), BF16), shape((t_rows, width), F32)] + [shape(g.shape, F32) for g in grads],
        in_specs=[in_hbm] * 6,
        out_specs=[in_hbm] * 6,
        scratch_shapes=[vm((t_rows, width), BF16), vm((t_rows, width), F32)] + [vm(g.shape, BF16) for g in grads]
        + [vm(g.shape, F32) for g in grads] + [dma((6,)), dma((6,))],
    )(*outs[:6])
    mine = gv[:8, :rows]
    return (layer_output[None], input_grad[None], mine[0], mine[1], g_qkv, mine[6], mine[7], g_out,
            mine[2], mine[3], mine[4], g_in, gv[16, :4 * rows], g_back, mine[5])


def solution(mesh):
    both = ("ctx", "fsdp")
    own, rows = P(both), P(both, None)
    seqs = P(("fsdp", "rep"), "ctx", None)
    in_specs = (seqs, P(("fsdp", "rep"), None), own, own, rows, own, own, rows, own, own, own, rows, own, rows, own, seqs)
    out_specs = (seqs, seqs, own, own, rows, own, own, rows, own, own, own, rows, own, rows, own)
    run = functools.partial(shards, mesh.shape["ctx"], mesh.shape["fsdp"])
    return jax.shard_map(run, mesh=mesh, in_specs=in_specs, out_specs=out_specs, check_vma=False)
```

```python
import functools

import jax
import jax.numpy as jnp
from jax import lax
from jax.experimental import pallas as pl
from jax.experimental.pallas import tpu as pltpu
from jax.sharding import PartitionSpec as P

H = 16
HD = 64
DOCS = 5
EPS = 1e-05
MASKED = -1e30
F32, BF16 = jnp.float32, jnp.bfloat16
MESH = pl.DeviceIdType.MESH
NN = ((1,), (0,))
NT = ((1,), (1,))
TN = ((0,), (0,))
QKV, OUT, IN, BACK, LATE = range(5)
CHUNK = 32


def dot(a, b, dims):
    return lax.dot_general(a, b, (dims, ((), ())), preferred_element_type=F32)


def norm_parts(x):
    center = x - jnp.mean(x, -1, keepdims=True)
    rstd = lax.rsqrt(jnp.mean(center * center, -1, keepdims=True) + EPS)
    return center * rstd, rstd


def norm_back(g, z, rstd, gain):
    gz = g * gain
    return rstd * (gz - jnp.mean(gz, -1, keepdims=True) - z * jnp.mean(gz * z, -1, keepdims=True))


def gelu_both(t):
    a, b = 0.7978845608028654, 0.044715
    t2 = t * t
    th = jnp.tanh(a * t * (1.0 + b * t2))
    half = 0.5 * (1.0 + th)
    return t * half, half + 0.5 * t * (1.0 - th * th) * (a * (1.0 + 3.0 * b * t2))


def fold(x):
    return jnp.sum(x.reshape(x.shape[0] // 8, 8, x.shape[1]), 0)


def body(dims, tok, cot_in, seg, pack, wq_hbm, wo_hbm, wi_hbm, wb_hbm,
         out_o, gx_o, gq_o, go_o, gi_o, gb_o, gv_o,
         wq, wo, wi, wb, packs, vecs, inb, n1, cot, n2, gbr, q_s, k_s, v_s, do_s, kt_s, vt_s, att, act, gpre, gproj,
         start_s, lse_s, delta_s, resid, gres, keep, tmp1, tmp2, snd, land,
         dk_s, dv_s, gwq, gwo, gwi, gwb, yq, yo, yi, yb, zq, zo, zi, zb, fq, fi, aq, ao, ai, ab,
         v6, v6r, vs, vz, ibg, sums,
         loc, pk_cs, pk_cr, pk_zs, pk_zr, wc_s, wc_r, wz_s, wz_r, wy_s, wy_r, ag_s, ag_r, rs_s, rs_r,
         gy_s, gy_r, gz_s, gz_r, gc_s, gc_r, gf_s, gf_r, vc_s, vc_r, vz_s, vz_r, out_s):
    n, nf, t_rows, width, rows, brows, ffc = dims
    half_w, half_f = width // 2, ffc // 2
    hc = width // n
    pw = hc // 2
    c, f, r = lax.axis_index("ctx"), lax.axis_index("fsdp"), lax.axis_index("rep")
    x, core = c // 2, c % 2

    def rel(d):
        return ((x + d // 2) % 2) * 2 + (core + d % 2) % 2

    def on_ctx(d):
        return (rel(d), f, r)

    def on_z(f2):
        return (c, f2, r)

    on_y = (c, f, 1 - r)
    ends = []

    def make(src, dst, ss, rs, dev):
        return pltpu.make_async_remote_copy(src_ref=src, dst_ref=dst, send_sem=ss, recv_sem=rs, device_id=dev,
                                            device_id_type=MESH)

    def send(src, dst, ss, rs, dev, cond=None):
        if cond is None:
            make(src, dst, ss, rs, dev).start()
            ends.append(lambda: make(src, dst, ss, rs, dev).wait_send())
        else:
            @pl.when(cond)
            def _():
                make(src, dst, ss, rs, dev).start()

            def end():
                @pl.when(cond)
                def _():
                    make(src, dst, ss, rs, dev).wait_send()
            ends.append(end)

    def arrived(dst, rs, dev):
        make(dst, dst, rs, rs, dev).wait_recv()

    def local(src, dst, sem):
        pltpu.make_async_copy(src, dst, sem).start()

    def local_done(dst, sem):
        pltpu.make_async_copy(dst, dst, sem).wait()

    for h in range(2):
        for j in range(3):
            local(wq_hbm.at[:, pl.ds(pl.multiple_of(j * width + c * hc + h * pw, pw), pw)],
                  wq.at[h, c, f, :, pl.ds(j * pw, pw)], loc.at[1])
        local(wo_hbm.at[:, pl.ds(h * half_w, half_w)], wo.at[h, f], loc.at[2])
        local(wb_hbm.at[:, pl.ds(h * half_w, half_w)], wb.at[h, f], loc.at[4])
    for h in range(2):
        local(wi_hbm.at[:, pl.ds(pl.multiple_of(c * ffc + h * half_f, half_f), half_f)], wi.at[h, c, f], loc.at[3])
    local(cot_in, cot.at[c], loc.at[0])
    packs[c, f] = pack[...]
    barrier = pltpu.get_barrier_semaphore()
    peers = [on_ctx(d) for d in (1, 2, 3)] + [on_z((f + s) % nf) for s in range(1, nf)] + [on_y]
    peers += [(c, (f + s) % nf, 1 - r) for s in range(1, nf)]
    for dev in peers:
        pl.semaphore_signal(barrier, inc=1, device_id=dev, device_id_type=MESH)
    pl.semaphore_wait(barrier, len(peers))

    for d in (1, 2, 3):
        send(packs.at[c, f], packs.at[c, f], pk_cs.at[d], pk_cr.at[c], on_ctx(d))

    def exchange(kind, hbm, buf, parts, step, w):
        for d in (2, 3, 1):
            c2 = rel(d)
            for h in range(2):
                for j in range(parts):
                    make(hbm.at[:, pl.ds(pl.multiple_of(j * width + c2 * step + h * w, w), w)],
                         buf.at[h, c, f, :, pl.ds(j * w, w)], wc_s.at[kind, d], wc_r.at[kind, c], on_ctx(d)).start()
            ends.append(lambda d=d: make(buf.at[:, c, f], buf.at[:, c, f], wc_s.at[kind, d], wc_r.at[kind, c],
                                         on_ctx(d)).wait_send())

    def exchanged(kind, buf):
        for d in (1, 2, 3):
            arrived(buf.at[:, rel(d), f], wc_r.at[kind, rel(d)], on_ctx(d))

    exchange(0, wq_hbm, wq, 3, hc, pw)
    exchange(1, wi_hbm, wi, 1, ffc, half_f)

    bufs = {QKV: wq, OUT: wo, IN: wi, BACK: wb}

    def block(buf, kind, h, f2):
        return buf.at[h, :, f2] if kind in (QKV, IN) else buf.at[h, f2]

    pieces = {QKV: 2, OUT: 1, IN: 2, BACK: 2}

    def part(kind, h, f2, p):
        buf = bufs[kind]
        if kind in (QKV, IN):
            return buf.at[h, pl.ds(p * (n // 2), n // 2), f2]
        return buf.at[h, f2] if kind == OUT else buf.at[h, f2, pl.ds(p * (brows // 2), brows // 2)]

    def w_z(kind, p, slot, src, dst, cond):
        b = part(kind, r, src, p)
        send(b, b, wz_s.at[kind, p, slot], wz_r.at[kind, p, src], on_z(dst), cond)

    def w_own(kind, p):
        for k, s in enumerate([1] + list(range(3, nf))):
            w_z(kind, p, 2 + 2 * k, f, f + s, f + s < nf)
            w_z(kind, p, 3 + 2 * k, f, f - s, f >= s)

    def sources(s):
        return (f - s, f >= s), (f + s, f + s < nf)

    def w_relay(kind, p):
        for way, (src, ok) in enumerate(sources(1)):
            w_z(kind, p, way, src, 2 * f - src, ok & ((f + 1 < nf) if way == 0 else (f >= 1)))

    def w_swap(kind, p, s):
        for src, ok in sources(s):
            b = part(kind, r, src, p)

            @pl.when(ok)
            def _():
                arrived(b, wz_r.at[kind, p, src], on_y)
            send(b, b, wy_s.at[kind, p, src], wy_r.at[kind, p, src], on_y, ok)

    def w_step(kind, p, s):
        if s == 3:
            for far in range(3, nf):
                w_swap(kind, p, far)
        elif s < nf:
            w_swap(kind, p, s)
            if s == 1:
                w_relay(kind, p)

    def w_arrived(kind):
        for p in range(pieces[kind]):
            for s in range(1, nf):
                f2 = (f + s) % nf
                arrived(part(kind, 1 - r, f2, p), wy_r.at[kind, p, f2], on_y)

    def ag_start(i, buf):
        for d, k in ((2, 0), (1, 1)):
            send(buf.at[c], buf.at[c], ag_s.at[i, k], ag_r.at[i, c], on_ctx(d))

    def ag_forward(i, buf):
        b = rel(2)
        arrived(buf.at[b], ag_r.at[i, b], on_ctx(2))
        send(buf.at[b], buf.at[b], ag_s.at[i, 2], ag_r.at[i, b], on_ctx(1))

    def ag_wait(i, buf, d):
        arrived(buf.at[rel(d)], ag_r.at[i, rel(d)], on_ctx(d))

    def rs_put(i, d, h, val):
        cols = pl.ds(h * half_w, half_w)
        if d == 0:
            keep[:, cols] = val
            return
        k = {3: 0, 2: 1, 1: 2}[d]
        if d == 2:
            arrived(land.at[i, 0, h], rs_r.at[i, 0, h], on_ctx(1))
            val = val + land[i, 0, h].astype(F32)
        snd[i % 2, k, h] = val.astype(BF16)
        make(snd.at[i % 2, k, h], land.at[i, k, h], rs_s.at[i, k, h], rs_r.at[i, k, h], on_ctx(2 if d == 2 else 1)).start()

    def rs_sent(i):
        for d, k in ((3, 0), (2, 1), (1, 2)):
            for h in range(2):
                make(snd.at[i % 2, k, h], land.at[i, k, h], rs_s.at[i, k, h], rs_r.at[i, k, h],
                     on_ctx(2 if d == 2 else 1)).wait_send()

    def rs_arrived(i):
        for h in range(2):
            arrived(land.at[i, 2, h], rs_r.at[i, 2, h], on_ctx(1))
            arrived(land.at[i, 1, h], rs_r.at[i, 1, h], on_ctx(2))

    def rs_rows(i, rw):
        parts = [keep[rw, pl.ds(h * half_w, half_w)] + land[i, 1, h, rw].astype(F32) + land[i, 2, h, rw].astype(F32)
                 for h in range(2)]
        return jnp.concatenate(parts, 1)

    def chunks(fn, init=0, size=CHUNK):
        return lax.fori_loop(0, t_rows // size, lambda i, v: fn(pl.ds(pl.multiple_of(i * size, size), size), v), init)

    sg = seg[...]
    start = jnp.zeros_like(sg)
    for doc in range(DOCS - 1):
        start = start + jnp.where(sg > doc, jnp.sum((sg == doc).astype(jnp.int32), -1, keepdims=True), 0)
    for b in range(n):
        start_s[b] = start[:, b * t_rows:(b + 1) * t_rows]

    local_done(wo.at[:, f], loc.at[2])
    w_own(OUT, 0)
    local_done(wb.at[:, f], loc.at[4])
    w_own(BACK, 0)
    for d in (1, 2, 3):
        arrived(packs.at[rel(d), f], pk_cr.at[rel(d)], on_ctx(d))
    for s in range(1, nf):
        f2 = (f + s) % nf
        send(packs.at[:, f], packs.at[:, f], pk_zs.at[s], pk_zr.at[f], on_z(f2))
    local_done(wq.at[:, c, f], loc.at[1])
    exchanged(0, wq)
    w_own(QKV, 0)
    w_own(QKV, 1)
    w_swap(OUT, 0, 1)
    w_swap(BACK, 0, 1)
    for s in range(1, nf):
        f2 = (f + s) % nf
        arrived(packs.at[:, f2], pk_zr.at[f2], on_z(f2))
    lane = lax.broadcasted_iota(jnp.int32, (8, 128), 1)
    per = 128 // rows
    for g in range(width // 128):
        acc = None
        for j in range(per):
            e = g * per + j
            piece = packs[e // nf, e % nf].astype(F32)[0:8]
            acc = piece if j == 0 else jnp.where(lane // rows == j, pltpu.roll(piece, j * rows, 1), acc)
        vecs[g] = acc
    for g in range(ffc // 128):
        acc = None
        for j in range(per):
            e = g * per + j
            k = e % 4
            piece = packs[c, e // 4].astype(F32)[8:16]
            piece = jnp.broadcast_to(piece[k:k + 1], (8, 128))
            acc = piece if j == 0 else jnp.where(lane // rows == j, pltpu.roll(piece, j * rows, 1), acc)
        inb[:, g * 128:(g + 1) * 128] = acc

    def vec(v):
        return jnp.concatenate([vecs[g, v:v + 1, :] for g in range(width // 128)], 1)

    def ln1(rw, _):
        z, _r = norm_parts(tok[rw].astype(F32))
        n1[c, rw] = (z * vec(0) + vec(1)).astype(BF16)
        return 0
    chunks(ln1)
    ag_start(0, n1)
    local_done(cot.at[c], loc.at[0])
    ag_start(1, cot)
    w_step(QKV, 0, 1)
    w_step(QKV, 1, 1)
    w_relay(OUT, 0)
    local_done(wi.at[:, c, f], loc.at[3])
    exchanged(1, wi)
    w_own(IN, 0)
    w_own(IN, 1)
    w_relay(BACK, 0)
    for s in (3, 2):
        w_step(QKV, 0, s)
        w_step(QKV, 1, s)
    w_step(OUT, 0, 3)
    w_step(OUT, 0, 2)
    ag_forward(0, n1)
    ag_wait(0, n1, 1)
    ag_wait(0, n1, 3)
    w_arrived(QKV)

    def project(b, _):
        for p in range(2):
            pr = dot(n1[b], wq[p].reshape(width, 3 * pw), NN)
            qv = ((pr[:, :pw] + vecs[c * 2 + p, 2:3, :]).astype(BF16).astype(F32) * (HD ** -0.5)).astype(BF16)
            kv = pr[:, pw:2 * pw].astype(BF16)
            vv = (pr[:, 2 * pw:] + vecs[c * 2 + p, 3:4, :]).astype(BF16)
            kt, vt = kv.T, vv.T
            for e in range(2):
                q_s[2 * p + e, b] = qv[:, e * HD:(e + 1) * HD]
                k_s[2 * p + e, b] = kv[:, e * HD:(e + 1) * HD]
                v_s[2 * p + e, b] = vv[:, e * HD:(e + 1) * HD]
                kt_s[2 * p + e, b] = kt[e * HD:(e + 1) * HD]
                vt_s[2 * p + e, b] = vt[e * HD:(e + 1) * HD]
        return 0
    lax.fori_loop(0, n, project, 0)

    key_row = lax.broadcasted_iota(jnp.int32, (t_rows, t_rows), 0)
    query_col = lax.broadcasted_iota(jnp.int32, (t_rows, t_rows), 1)

    def allowed(qb, kb, diagonal):
        ok = key_row >= start_s[qb] - kb * t_rows
        return ok & (key_row <= query_col) if diagonal else ok

    def scores(h, qb, kb, ok):
        return jnp.where(ok, dot(k_s[h, kb], q_s[h, qb], NT), MASKED)

    def attend(heads, qb):
        def step(kb, carry, diagonal=False):
            ok = allowed(qb, kb, diagonal)
            out = []
            for h, (m, l, acc) in zip(heads, carry):
                s = scores(h, qb, kb, ok)
                m2 = jnp.maximum(m, jnp.max(s, 0, keepdims=True))
                p = jnp.exp(s - m2)
                a = jnp.exp(m - m2)
                out.append((m2, l * a + jnp.sum(p, 0, keepdims=True), acc * a + dot(vt_s[h, kb], p.astype(BF16), NN)))
            return tuple(out)
        zero = jnp.zeros((1, t_rows), F32)
        carry = lax.fori_loop(0, qb, step, tuple((zero + MASKED, zero, jnp.zeros((HD, t_rows), F32)) for _ in heads))
        for h, (m, l, acc) in zip(heads, step(qb, carry, True)):
            att[qb, h] = (acc / l).astype(BF16)
            lse_s[h, qb] = m + jnp.log(l)

    polls = [[(IN, 0, 1), (BACK, 0, 3)], [(IN, 1, 1)], [(IN, 0, 3), (BACK, 0, 2)], [(IN, 1, 3)], [(IN, 0, 2)], [(IN, 1, 2)],
             [(BACK, 1, 1)], [(BACK, 1, 3)]]
    for d in (3, 2, 1, 0):
        qb = rel(d)
        for k in range(2):
            attend((2 * k, 2 * k + 1), qb)
            for poll in polls[2 * (3 - d) + k]:
                w_step(*poll)
            if d == 3 and k == 1:
                w_own(BACK, 1)
        if d == 3:
            w_arrived(OUT)
        if d == 2:
            ag_forward(1, cot)
        for h in range(2):
            rs_put(0, d, h, dot(att[qb].reshape(hc, t_rows), wo[h].reshape(hc, half_w), TN))
    rs_arrived(0)

    def ln2(rw, _):
        res = tok[rw].astype(F32) + rs_rows(0, rw) + vec(4)
        resid[rw] = res
        z, _r = norm_parts(res)
        n2[c, rw] = (z * vec(5) + vec(6)).astype(BF16)
        return 0
    chunks(ln2)
    ag_start(2, n2)
    w_step(BACK, 1, 2)
    w_arrived(IN)

    for d in (0, 1, 3, 2):
        b = rel(d)
        if d == 1:
            ag_wait(2, n2, 1)
        if d == 3:
            ag_forward(2, n2)
            ag_wait(2, n2, 3)

        def up(j, _):
            tmp1[...] = dot(n2[b], wi[j].reshape(width, half_f), NN)
            cols = pl.ds(pl.multiple_of(j * half_f, half_f), half_f)
            bias = inb[0:1, cols]

            def one(rw, _):
                a, da = gelu_both(tmp1[rw] + bias)
                act[b, rw, cols] = a.astype(BF16)
                gpre[b, rw, cols] = da.astype(BF16)
                return 0
            chunks(one)
            return 0
        lax.fori_loop(0, 2, up, 0)
    rs_sent(0)
    ag_wait(1, cot, 1)
    ag_wait(1, cot, 3)

    grads = {OUT: (gwo, yo, zo), IN: (gwi, yi, zi), BACK: (gwb, yb, zb)}
    alls = {QKV: aq.at[0], LATE: aq.at[1], OUT: ao, IN: ai, BACK: ab}
    nh = n // 2

    def g_part(kind, r2, f2):
        if kind in (QKV, LATE):
            return gwq.at[kind // LATE, pl.ds(r2 * nh, nh), f2]
        return block(grads[kind][0], kind, r2, f2)

    def y_part(kind, f2):
        if kind in (QKV, LATE):
            return yq.at[kind // LATE, :, f2]
        return grads[kind][1].at[:, f2] if kind == IN else grads[kind][1].at[f2]

    def z_part(kind, f2):
        return zq.at[kind // LATE, f2] if kind in (QKV, LATE) else grads[kind][2].at[f2]

    def g_y(kind):
        for s in (*range(1, nf), 0):
            f2 = (f + s) % nf
            send(g_part(kind, 1 - r, f2), y_part(kind, f2), gy_s.at[kind, f2], gy_r.at[kind, f2], on_y)

    def g_z(kind, s):
        f2 = (f + s) % nf
        g, y = g_part(kind, r, f2), y_part(kind, f2)
        arrived(y, gy_r.at[kind, f2], on_y)
        if kind in (OUT, BACK):
            g[...] = (g[...].astype(F32) + y[...].astype(F32)).astype(BF16)
        else:
            for i in range(y.shape[0]):
                g[i] = (g[i].astype(F32) + y[i].astype(F32)).astype(BF16)
        if s:
            send(g, z_part(kind, f), gz_s.at[kind, s], gz_r.at[kind, f], on_z(f2))

    def g_rest(kind, s0):
        for s in (*range(s0, nf), 0):
            g_z(kind, s)

    def g_f(kind):
        for s in range(1, nf):
            f2 = (f + s) % nf
            arrived(z_part(kind, f2), gz_r.at[kind, f2], on_z(f2))
        g = g_part(kind, r, f)
        zs = [z_part(kind, (f + s) % nf) for s in range(1, nf)]
        if kind in (OUT, BACK):
            tot = g[...].astype(F32)
            for z in zs:
                tot = tot + z[...].astype(F32)
            alls[kind][r] = tot.astype(BF16)
            send(alls[kind].at[r], alls[kind].at[r], gf_s.at[kind], gf_r.at[kind], on_y)
            return
        fin = fi if kind == IN else fq.at[kind // LATE]
        for i in range(fin.shape[0]):
            tot = g[i].astype(F32)
            for z in zs:
                tot = tot + z[i].astype(F32)
            fin[i] = tot.astype(BF16)
        if kind == IN:
            for d in (2, 3, 1):
                send(fin.at[rel(d)], ai.at[r, c], gc_s.at[kind, d], gc_r.at[kind, c], on_ctx(d))
            ai[r, c] = fin[c]
            return
        for i in range(nh):
            owner = r * nh + i
            send(fin.at[i], alls[kind].at[c], gc_s.at[kind, i], gc_r.at[kind, c], (owner, f, r), owner != c)

            @pl.when(owner == c)
            def _():
                alls[kind][c] = fin[i]

    def g_e(kind):
        a = alls[kind]
        if kind == IN:
            for d in (1, 2, 3):
                arrived(a.at[r, rel(d)], gc_r.at[kind, rel(d)], on_ctx(d))
            send(a.at[r], a.at[r], gf_s.at[kind], gf_r.at[kind], on_y)
            return

        @pl.when(c // nh == r)
        def _():
            for d in (1, 2, 3):
                arrived(a.at[rel(d)], gc_r.at[kind, rel(d)], on_ctx(d))
        send(a, a, gf_s.at[kind], gf_r.at[kind], on_y, c // nh == r)

    def g_out(kind):
        a = alls[kind]
        if kind in (QKV, LATE):
            @pl.when(c // nh != r)
            def _():
                arrived(a, gf_r.at[kind], on_y)
            h = kind // LATE
            for c2 in range(n):
                for j in range(3):
                    local(a.at[c2, :, pl.ds(j * pw, pw)], gq_o.at[:, pl.ds(j * width + c2 * hc + h * pw, pw)], out_s.at[kind])
            return
        arrived(a.at[1 - r], gf_r.at[kind], on_y)
        for h in range(2):
            if kind == IN:
                for c2 in range(n):
                    local(a.at[h, c2], gi_o.at[:, pl.ds(c2 * ffc + h * half_f, half_f)], out_s.at[kind])
            else:
                local(a.at[h], (go_o if kind == OUT else gb_o).at[:, pl.ds(h * half_w, half_w)], out_s.at[kind])

    def whole(buf, cols):
        v = buf[:, :, cols]
        return v.reshape(n * t_rows, v.shape[2])

    def grad_back(h):
        per_f = ffc // nf
        tiles = max(1, 256 // per_f)

        def one(i, _):
            a = whole(act, pl.ds(pl.multiple_of(i * 256, 256), 256))
            g = whole(cot, pl.ds(pl.multiple_of(h * half_w, half_w), half_w))
            v = dot(a, g, TN).astype(BF16)
            gwb[h, pl.ds(i * tiles, tiles)] = v.reshape(tiles, per_f, half_w)
            return 0
        lax.fori_loop(0, ffc // 256, one, 0)

    def grad_in(h):
        def one(i, _):
            a = whole(n2, pl.ds(pl.multiple_of(i * hc, hc), hc))
            g = whole(gpre, pl.ds(pl.multiple_of(h * half_f, half_f), half_f))
            gwi[h, i] = dot(a, g, TN).astype(BF16).reshape(nf, rows, half_f)
            return 0
        lax.fori_loop(0, n, one, 0)

    grad_back(1 - r)
    g_y(BACK)
    grad_back(r)
    w_arrived(BACK)

    ibg[...] = jnp.zeros_like(ibg)
    for d in (3, 2, 1, 0):
        b = rel(d)

        def slope(j, _):
            wide = jnp.concatenate([wb[h, pl.ds(j * (nf // 2), nf // 2)].reshape(half_f, half_w) for h in range(2)], 1)
            tmp2[...] = dot(cot[b], wide, NT)
            cols = pl.ds(pl.multiple_of(j * half_f, half_f), half_f)

            def one(rw, acc):
                gp = (tmp2[rw] * gpre[b, rw, cols].astype(F32)).astype(BF16)
                gpre[b, rw, cols] = gp
                return acc + fold(gp.astype(F32))
            ibg[j] += chunks(one, jnp.zeros((8, half_f), F32))
            return 0
        lax.fori_loop(0, 2, slope, 0)
        for h in range(2):
            wide = jnp.concatenate([wi[j, pl.ds(h * (n // 2), n // 2)].reshape(half_w, half_f) for j in range(2)], 1)
            rs_put(1, d, h, dot(gpre[b], wide, NT))
    grad_in(1 - r)
    g_y(IN)
    g_z(BACK, 1)
    grad_in(r)
    rs_arrived(1)

    def ln2_back(rw, accs):
        gain, shift, bb, ob = accs
        g = rs_rows(1, rw)
        z, rstd = norm_parts(resid[rw])
        ct = cot[c, rw].astype(F32)
        gr = ct + norm_back(g, z, rstd, vec(5))
        gres[rw] = gr
        low = gr.astype(BF16)
        gbr[c, rw] = low
        return gain + fold(g * z), shift + fold(g), bb + fold(ct), ob + fold(low.astype(F32))
    zero8 = jnp.zeros((8, width), F32)
    accs = chunks(ln2_back, (zero8, zero8, zero8, zero8), 16)
    for i, a in zip((3, 4, 5, 2), accs):
        sums[i] = a
    ag_start(3, gbr)
    if nf > 2:
        g_z(BACK, 2)

    for d in (3, 2, 1, 0):
        for h in range(2):
            rs_put(2, d, h, dot(act[rel(d)], wb[h].reshape(ffc, half_w), NN))
    ag_wait(3, gbr, 1)

    def near(t):
        return rel(t ^ (t // 2))

    def g_attended(t, _):
        b = near(t)
        wide = jnp.concatenate([wo[h].reshape(hc, half_w) for h in range(2)], 1)
        g = dot(gbr[b], wide, NT).astype(BF16)
        gt = g.T.astype(F32).reshape(H // n, HD, t_rows)
        for h in range(H // n):
            do_s[h, b] = g[:, h * HD:(h + 1) * HD]
            delta_s[h, b] = jnp.sum(gt[h] * att[b, h].astype(F32), 0, keepdims=True)
        return 0
    lax.fori_loop(0, 2, g_attended, 0)

    def grad_out(h):
        tot = jnp.zeros((hc, half_w), F32)
        cols = pl.ds(pl.multiple_of(h * half_w, half_w), half_w)
        for b in range(n):
            tot = tot + dot(att[b].reshape(hc, t_rows), gbr[b, :, cols], NN)
        gwo[h] = tot.astype(BF16).reshape(nf, rows, half_w)

    def finish_out(rw, _):
        out_o[rw] = (resid[rw] + rs_rows(2, rw) + vec(7)).astype(BF16)
        return 0

    def pair_blocks(p, lo, hi):
        def one(t, _):
            qb = near(t)

            def step(kb, dqts, diagonal=False):
                ok = allowed(qb, kb, diagonal)
                out = []
                for e in range(2):
                    h = 2 * p + e
                    q, do = q_s[h, qb], do_s[h, qb]
                    pr = jnp.exp(scores(h, qb, kb, ok) - lse_s[h, qb])
                    dp = dot(v_s[h, kb], do, NT)
                    ds = (pr * (dp - delta_s[h, qb])).astype(BF16)
                    dv_s[e, kb] += dot(pr.astype(BF16), do, NN)
                    dk_s[e, kb] += dot(ds, q, NN)
                    out.append(dqts[e] + dot(kt_s[h, kb], ds, NN))
                return tuple(out)
            dqts = lax.fori_loop(0, qb, step, (jnp.zeros((HD, t_rows), F32),) * 2)
            for e, dqt in enumerate(step(qb, dqts, True)):
                gproj[p, qb, :, e * HD:(e + 1) * HD] = (dqt * (HD ** -0.5)).T.astype(BF16)
            return 0
        lax.fori_loop(lo, hi, one, 0)

    def pair_start():
        dk_s[...] = jnp.zeros_like(dk_s)
        dv_s[...] = jnp.zeros_like(dv_s)

    def pair_end(p):
        for e in range(2):
            for b in range(n):
                gproj[p, b, :, pw + e * HD:pw + (e + 1) * HD] = dk_s[e, b].astype(BF16)
                gproj[p, b, :, 2 * pw + e * HD:2 * pw + (e + 1) * HD] = dv_s[e, b].astype(BF16)

        def grad_qkv(i, _):
            a = whole(n1, pl.ds(pl.multiple_of(i * hc, hc), hc))
            gwq[p, i] = dot(a, gproj[p].reshape(n * t_rows, 3 * pw), TN).astype(BF16).reshape(nf, rows, 3 * pw)
            return 0
        lax.fori_loop(0, n, grad_qkv, 0)

    pair_start()
    pair_blocks(0, 0, 2)
    g_rest(BACK, 3)
    ag_forward(3, gbr)
    ag_wait(3, gbr, 3)
    lax.fori_loop(2, n, g_attended, 0)
    pair_blocks(0, 2, n)
    g_z(IN, 1)
    pair_end(0)
    g_y(QKV)
    grad_out(1 - r)
    g_y(OUT)
    grad_out(r)
    rs_arrived(2)
    chunks(finish_out)
    if nf > 2:
        g_z(IN, 2)
    pair_start()
    pair_blocks(1, 0, 2)
    g_rest(IN, 3)
    pair_blocks(1, 2, n)
    g_z(QKV, 1)
    if nf > 2:
        g_z(QKV, 2)
    pair_end(1)
    g_y(LATE)
    g_rest(QKV, 3)
    rs_sent(1)
    for d in (3, 2, 1, 0):
        for h in range(2):
            gp = jnp.concatenate([gproj[p, rel(d)] for p in range(2)], 1)
            wide = jnp.concatenate([wq[p, pl.ds(h * (n // 2), n // 2)].reshape(half_w, 3 * pw) for p in range(2)], 1)
            rs_put(3, d, h, dot(gp, wide, NT))
    g_f(IN)
    g_f(BACK)
    g_rest(OUT, 1)
    g_rest(LATE, 1)
    g_f(QKV)
    g_e(IN)
    rs_arrived(3)

    def ln1_back(rw, accs):
        gain, shift = accs
        g = rs_rows(3, rw)
        z, rstd = norm_parts(tok[rw].astype(F32))
        gx_o[rw] = gres[rw] + norm_back(g, z, rstd, vec(0))
        return gain + fold(g * z), shift + fold(g)
    accs = chunks(ln1_back, (zero8, zero8), 16)
    sums[0], sums[1] = accs[0], accs[1]

    g_e(QKV)
    g_f(OUT)
    for i in range(8):
        row = jnp.sum(sums[i], 0, keepdims=True) if i < 6 else jnp.zeros((1, width), F32)
        for c2 in range(n):
            v6[c2, i:i + 1, :] = row[:, c2 * hc:(c2 + 1) * hc]
    for d in (1, 2, 3):
        send(v6.at[rel(d)], v6r.at[c], vc_s.at[d], vc_r.at[c], on_ctx(d))
    vs[...] = jnp.zeros_like(vs)
    for p in range(2):
        gsum = jnp.sum(gproj[p].reshape(n * t_rows, 3 * pw).astype(F32), 0, keepdims=True)
        v6[c, 6:7, p * pw:(p + 1) * pw] = gsum[:, :pw]
        v6[c, 7:8, p * pw:(p + 1) * pw] = gsum[:, 2 * pw:]
    for j in range(2):
        row = jnp.sum(ibg[j], 0, keepdims=True)
        for k in range(2):
            i = 8 + 2 * j + k
            vs[i:i + 1, :] = row[:, k * hc:(k + 1) * hc]
    for d in (1, 2, 3):
        arrived(v6r.at[rel(d)], vc_r.at[rel(d)], on_ctx(d))
    vs[0:8] = v6[c] + v6r[rel(1)] + v6r[rel(2)] + v6r[rel(3)]
    me = r * nf + f
    vz[me] = vs[...]
    for k in range(1, 2 * nf):
        f2, r2 = (f + k) % nf, (r + k // nf) % 2
        send(vs, vz.at[me], vz_s.at[k], vz_r.at[me], (c, f2, r2))
    g_f(LATE)
    g_e(LATE)
    g_out(BACK)
    g_out(OUT)
    for k in range(1, 2 * nf):
        f2, r2 = (f + k) % nf, (r + k // nf) % 2
        arrived(vz.at[r2 * nf + f2], vz_r.at[r2 * nf + f2], (c, f2, r2))
    tot = vz[0]
    for k in range(1, 2 * nf):
        tot = tot + vz[k]
    mine, mine_in = tot[:, :rows], tot[8:9, :4 * rows]
    for f2 in range(1, nf):
        row, lo = 8 + f2 * 4 * rows // hc, f2 * 4 * rows % hc
        mine = jnp.where(f == f2, tot[:, f2 * rows:(f2 + 1) * rows], mine)
        mine_in = jnp.where(f == f2, tot[row:row + 1, lo:lo + 4 * rows], mine_in)
    gv_o[0:16, :rows] = mine
    gv_o[16:17, :4 * rows] = mine_in
    g_out(IN)
    g_out(QKV)
    g_out(LATE)
    rs_sent(2)
    rs_sent(3)
    for end in ends:
        end()
    for kind in range(5):
        local_done(alls[kind], out_s.at[kind])


def finish(lo_i, gx_i, gq_i, go_i, gi_i, gb_i, lo_o, gx_o, gq_o, go_o, gi_o, gb_o,
           lo_b, gx_b, gq_b, go_b, gi_b, gb_b, gq_w, go_w, gi_w, gb_w, sem_i, sem_o):
    parts = [(gb_i, gb_b, gb_w, gb_o), (gi_i, gi_b, gi_w, gi_o), (gq_i, gq_b, gq_w, gq_o), (go_i, go_b, go_w, go_o),
             (gx_i, gx_b, gx_b, gx_o), (lo_i, lo_b, lo_b, lo_o)]
    for k, (src, low, wide, dst) in enumerate(parts):
        pltpu.make_async_copy(src, low, sem_i.at[k]).start()
    for k, (src, low, wide, dst) in enumerate(parts):
        pltpu.make_async_copy(src, low, sem_i.at[k]).wait()
        if wide is not low:
            wide[...] = low[...].astype(F32)
        pltpu.make_async_copy(wide, dst, sem_o.at[k]).start()
    for k, (src, low, wide, dst) in enumerate(parts):
        pltpu.make_async_copy(wide, dst, sem_o.at[k]).wait()


def shards(n, nf, tokens, segments, ln1_gain, ln1_bias, w_qkv, q_bias, v_bias, w_out, out_bias,
           ln2_gain, ln2_bias, w_in, in_bias, w_back, back_bias, cotangent):
    t_rows, width = tokens.shape[1], tokens.shape[2]
    rows, brows = w_qkv.shape[0], w_back.shape[0]
    ffc = w_in.shape[1] // n
    slots = segments.shape[1]
    heads = H // n
    hc, half_w, half_f = width // n, width // 2, ffc // 2
    q3 = 3 * hc // 2
    small = jnp.stack([ln1_gain, ln1_bias, q_bias, v_bias, out_bias, ln2_gain, ln2_bias, back_bias])
    small = jnp.concatenate([small, in_bias.reshape(4, rows), jnp.zeros((4, rows), BF16)], 0)
    small = jnp.pad(small, ((0, 0), (0, 128 - rows)))
    dims = (n, nf, t_rows, width, rows, brows, ffc)
    vm = pltpu.VMEM
    dma = pltpu.SemaphoreType.DMA
    per_head = (heads, n, t_rows, HD)
    per_head_t = (heads, n, HD, t_rows)
    scratch = [
        vm((2, n, nf, rows, q3), BF16), vm((2, nf, rows, half_w), BF16), vm((2, n, nf, rows, half_f), BF16),
        vm((2, nf, brows, half_w), BF16), vm((n, nf, 16, 128), BF16), vm((width // 128, 8, 128), F32), vm((8, ffc), F32),
        vm((n, t_rows, width), BF16), vm((n, t_rows, width), BF16), vm((n, t_rows, width), BF16), vm((n, t_rows, width), BF16),
        vm(per_head, BF16), vm(per_head, BF16), vm(per_head, BF16), vm(per_head, BF16), vm(per_head_t, BF16), vm(per_head_t, BF16),
        vm((n, heads, HD, t_rows), BF16), vm((n, t_rows, ffc), BF16), vm((n, t_rows, ffc), BF16), vm((2, n, t_rows, q3), BF16),
        vm((n, 1, t_rows), jnp.int32), vm((heads, n, 1, t_rows), F32), vm((heads, n, 1, t_rows), F32),
        vm((t_rows, width), F32), vm((t_rows, width), F32), vm((t_rows, width), F32), vm((t_rows, half_f), F32), vm((t_rows, half_f), F32),
        vm((2, 3, 2, t_rows, half_w), BF16), vm((4, 3, 2, t_rows, half_w), BF16),
        vm((2, n, t_rows, HD), F32), vm((2, n, t_rows, HD), F32),
        vm((2, n, nf, rows, q3), BF16), vm((2, nf, rows, half_w), BF16), vm((2, n, nf, rows, half_f), BF16), vm((2, nf, brows, half_w), BF16),
        vm((2, n // 2, nf, rows, q3), BF16), vm((nf, rows, half_w), BF16), vm((n, nf, rows, half_f), BF16), vm((nf, brows, half_w), BF16),
        vm((2, nf, n // 2, rows, q3), BF16), vm((nf, rows, half_w), BF16), vm((nf, n, rows, half_f), BF16), vm((nf, brows, half_w), BF16),
        vm((2, n // 2, rows, q3), BF16), vm((n, rows, half_f), BF16),
        vm((2, n, rows, q3), BF16), vm((2, rows, half_w), BF16), vm((2, n, rows, half_f), BF16), vm((2, brows, half_w), BF16),
        vm((n, 8, hc), F32), vm((n, 8, hc), F32), vm((16, hc), F32), vm((2 * nf, 16, hc), F32),
        vm((2, 8, half_f), F32), vm((8, 8, width), F32),
        dma((5,)), dma((4,)), dma((n,)), dma((nf,)), dma((nf,)), dma((2, 4)), dma((2, n)),
        dma((4, 2, 4 + 2 * max(0, nf - 3))), dma((4, 2, nf)), dma((4, 2, nf)), dma((4, 2, nf)), dma((4, 3)), dma((4, n)), dma((4, 3, 2)), dma((4, 3, 2)),
        dma((5, nf)), dma((5, nf)), dma((5, nf)), dma((5, nf)), dma((5, 4)), dma((5, n)), dma((5,)), dma((5,)),
        dma((4,)), dma((n,)), dma((2 * nf,)), dma((2 * nf,)), dma((5,)),
    ]
    shape = jax.ShapeDtypeStruct
    in_vmem, in_hbm = pl.BlockSpec(memory_space=vm), pl.BlockSpec(memory_space=pl.ANY)
    outs = pl.pallas_call(
        functools.partial(body, dims),
        out_shape=[shape((t_rows, width), BF16), shape((t_rows, width), F32), shape(w_qkv.shape, BF16), shape(w_out.shape, BF16),
                   shape(w_in.shape, BF16), shape(w_back.shape, BF16), shape((24, hc), F32)],
        in_specs=[in_vmem, in_hbm, in_vmem, in_vmem] + [in_hbm] * 4,
        out_specs=[in_vmem] * 2 + [in_hbm] * 4 + [in_vmem],
        scratch_shapes=scratch,
        compiler_params=pltpu.CompilerParams(collective_id=0, has_side_effects=True, vmem_limit_bytes=67043328),
    )(tokens[0], cotangent[0], segments, small, w_qkv, w_out, w_in, w_back)
    gv = outs[6]
    grads = [w_qkv, w_out, w_in, w_back]
    layer_output, input_grad, g_qkv, g_out, g_in, g_back = pl.pallas_call(
        finish,
        out_shape=[shape((t_rows, width), BF16), shape((t_rows, width), F32)] + [shape(g.shape, F32) for g in grads],
        in_specs=[in_hbm] * 6,
        out_specs=[in_hbm] * 6,
        scratch_shapes=[vm((t_rows, width), BF16), vm((t_rows, width), F32)] + [vm(g.shape, BF16) for g in grads]
        + [vm(g.shape, F32) for g in grads] + [dma((6,)), dma((6,))],
    )(*outs[:6])
    mine = gv[:8, :rows]
    return (layer_output[None], input_grad[None], mine[0], mine[1], g_qkv, mine[6], mine[7], g_out,
            mine[2], mine[3], mine[4], g_in, gv[16, :4 * rows], g_back, mine[5])


def solution(mesh):
    both = ("ctx", "fsdp")
    own, rows = P(both), P(both, None)
    seqs = P(("fsdp", "rep"), "ctx", None)
    in_specs = (seqs, P(("fsdp", "rep"), None), own, own, rows, own, own, rows, own, own, own, rows, own, rows, own, seqs)
    out_specs = (seqs, seqs, own, own, rows, own, own, rows, own, own, own, rows, own, rows, own)
    run = functools.partial(shards, mesh.shape["ctx"], mesh.shape["fsdp"])
    return jax.shard_map(run, mesh=mesh, in_specs=in_specs, out_specs=out_specs, check_vma=False)
```

```python
import functools

import jax
import jax.numpy as jnp
from jax import lax
from jax.experimental import pallas as pl
from jax.experimental.pallas import tpu as pltpu
from jax.sharding import PartitionSpec as P

H = 16
HD = 64
DOCS = 5
EPS = 1e-05
MASKED = -1e30
F32, BF16 = jnp.float32, jnp.bfloat16
MESH = pl.DeviceIdType.MESH
NN = ((1,), (0,))
NT = ((1,), (1,))
TN = ((0,), (0,))
QKV, OUT, IN, BACK, LATE = range(5)
CHUNK = 32


def dot(a, b, dims):
    return lax.dot_general(a, b, (dims, ((), ())), preferred_element_type=F32)


def norm_parts(x):
    center = x - jnp.mean(x, -1, keepdims=True)
    rstd = lax.rsqrt(jnp.mean(center * center, -1, keepdims=True) + EPS)
    return center * rstd, rstd


def norm_back(g, z, rstd, gain):
    gz = g * gain
    return rstd * (gz - jnp.mean(gz, -1, keepdims=True) - z * jnp.mean(gz * z, -1, keepdims=True))


def gelu_both(t):
    a, b = 0.7978845608028654, 0.044715
    t2 = t * t
    th = jnp.tanh(a * t * (1.0 + b * t2))
    half = 0.5 * (1.0 + th)
    return t * half, half + 0.5 * t * (1.0 - th * th) * (a * (1.0 + 3.0 * b * t2))


def fold(x):
    return jnp.sum(x.reshape(x.shape[0] // 8, 8, x.shape[1]), 0)


def body(dims, tok, cot_in, seg, pack, wq_hbm, wo_hbm, wi_hbm, wb_hbm,
         out_o, gx_o, gq_o, go_o, gi_o, gb_o, gv_o,
         wq, wo, wi, wb, packs, vecs, inb, n1, cot, n2, gbr, q_s, k_s, v_s, do_s, kt_s, vt_s, att, act, gpre, gproj,
         start_s, lse_s, delta_s, resid, gres, keep, tmp1, tmp2, snd, land,
         dk_s, dv_s, gwq, gwo, gwi, gwb, yq, yo, yi, yb, zq, zo, zi, zb, fq, fi, aq, ao, ai, ab,
         v6, v6r, vs, vz, ibg, sums,
         loc, pk_cs, pk_cr, pk_zs, pk_zr, wc_s, wc_r, wz_s, wz_r, wy_s, wy_r, ag_s, ag_r, rs_s, rs_r,
         gy_s, gy_r, gz_s, gz_r, gc_s, gc_r, gf_s, gf_r, vc_s, vc_r, vz_s, vz_r, out_s):
    n, nf, t_rows, width, rows, brows, ffc = dims
    half_w, half_f = width // 2, ffc // 2
    hc = width // n
    pw = hc // 2
    c, f, r = lax.axis_index("ctx"), lax.axis_index("fsdp"), lax.axis_index("rep")
    x, core = c // 2, c % 2

    def rel(d):
        return ((x + d // 2) % 2) * 2 + (core + d % 2) % 2

    def on_ctx(d):
        return (rel(d), f, r)

    def on_z(f2):
        return (c, f2, r)

    on_y = (c, f, 1 - r)
    ends = []

    def make(src, dst, ss, rs, dev):
        return pltpu.make_async_remote_copy(src_ref=src, dst_ref=dst, send_sem=ss, recv_sem=rs, device_id=dev,
                                            device_id_type=MESH)

    def send(src, dst, ss, rs, dev, cond=None):
        if cond is None:
            make(src, dst, ss, rs, dev).start()
            ends.append(lambda: make(src, dst, ss, rs, dev).wait_send())
        else:
            @pl.when(cond)
            def _():
                make(src, dst, ss, rs, dev).start()

            def end():
                @pl.when(cond)
                def _():
                    make(src, dst, ss, rs, dev).wait_send()
            ends.append(end)

    def arrived(dst, rs, dev):
        make(dst, dst, rs, rs, dev).wait_recv()

    def local(src, dst, sem):
        pltpu.make_async_copy(src, dst, sem).start()

    def local_done(dst, sem):
        pltpu.make_async_copy(dst, dst, sem).wait()

    for h in range(2):
        for j in range(3):
            local(wq_hbm.at[:, pl.ds(pl.multiple_of(j * width + c * hc + h * pw, pw), pw)],
                  wq.at[h, c, f, :, pl.ds(j * pw, pw)], loc.at[1])
        local(wo_hbm.at[:, pl.ds(h * half_w, half_w)], wo.at[h, f], loc.at[2])
        local(wb_hbm.at[:, pl.ds(h * half_w, half_w)], wb.at[h, f], loc.at[4])
    for h in range(2):
        local(wi_hbm.at[:, pl.ds(pl.multiple_of(c * ffc + h * half_f, half_f), half_f)], wi.at[h, c, f], loc.at[3])
    local(cot_in, cot.at[c], loc.at[0])
    packs[c, f] = pack[...]
    barrier = pltpu.get_barrier_semaphore()
    peers = [on_ctx(d) for d in (1, 2, 3)] + [on_z((f + s) % nf) for s in range(1, nf)] + [on_y]
    peers += [(c, (f + s) % nf, 1 - r) for s in range(1, nf)]
    for dev in peers:
        pl.semaphore_signal(barrier, inc=1, device_id=dev, device_id_type=MESH)
    pl.semaphore_wait(barrier, len(peers))

    for d in (1, 2, 3):
        send(packs.at[c, f], packs.at[c, f], pk_cs.at[d], pk_cr.at[c], on_ctx(d))

    def exchange(kind, hbm, buf, parts, step, w):
        for d in (2, 3, 1):
            c2 = rel(d)
            for h in range(2):
                for j in range(parts):
                    make(hbm.at[:, pl.ds(pl.multiple_of(j * width + c2 * step + h * w, w), w)],
                         buf.at[h, c, f, :, pl.ds(j * w, w)], wc_s.at[kind, d], wc_r.at[kind, c], on_ctx(d)).start()
            ends.append(lambda d=d: make(buf.at[:, c, f], buf.at[:, c, f], wc_s.at[kind, d], wc_r.at[kind, c],
                                         on_ctx(d)).wait_send())

    def exchanged(kind, buf):
        for d in (1, 2, 3):
            arrived(buf.at[:, rel(d), f], wc_r.at[kind, rel(d)], on_ctx(d))

    exchange(0, wq_hbm, wq, 3, hc, pw)
    exchange(1, wi_hbm, wi, 1, ffc, half_f)

    bufs = {QKV: wq, OUT: wo, IN: wi, BACK: wb}

    def block(buf, kind, h, f2):
        return buf.at[h, :, f2] if kind in (QKV, IN) else buf.at[h, f2]

    pieces = {QKV: 2, OUT: 1, IN: 2, BACK: 2}

    def part(kind, h, f2, p):
        buf = bufs[kind]
        if kind in (QKV, IN):
            return buf.at[h, pl.ds(p * (n // 2), n // 2), f2]
        return buf.at[h, f2] if kind == OUT else buf.at[h, f2, pl.ds(p * (brows // 2), brows // 2)]

    def w_z(kind, p, slot, src, dst, cond):
        b = part(kind, r, src, p)
        send(b, b, wz_s.at[kind, p, slot], wz_r.at[kind, p, src], on_z(dst), cond)

    def w_own(kind, p):
        for k, s in enumerate([1] + list(range(3, nf))):
            w_z(kind, p, 2 + 2 * k, f, f + s, f + s < nf)
            w_z(kind, p, 3 + 2 * k, f, f - s, f >= s)

    def sources(s):
        return (f - s, f >= s), (f + s, f + s < nf)

    def w_relay(kind, p):
        for way, (src, ok) in enumerate(sources(1)):
            w_z(kind, p, way, src, 2 * f - src, ok & ((f + 1 < nf) if way == 0 else (f >= 1)))

    def w_swap(kind, p, s):
        for src, ok in sources(s):
            b = part(kind, r, src, p)

            @pl.when(ok)
            def _():
                arrived(b, wz_r.at[kind, p, src], on_y)
            send(b, b, wy_s.at[kind, p, src], wy_r.at[kind, p, src], on_y, ok)

    def w_step(kind, p, s):
        if s == 3:
            for far in range(3, nf):
                w_swap(kind, p, far)
        elif s < nf:
            w_swap(kind, p, s)
            if s == 1:
                w_relay(kind, p)

    def w_arrived(kind):
        for p in range(pieces[kind]):
            for s in range(1, nf):
                f2 = (f + s) % nf
                arrived(part(kind, 1 - r, f2, p), wy_r.at[kind, p, f2], on_y)

    def ag_start(i, buf):
        for d, k in ((2, 0), (1, 1)):
            send(buf.at[c], buf.at[c], ag_s.at[i, k], ag_r.at[i, c], on_ctx(d))

    def ag_forward(i, buf):
        b = rel(2)
        arrived(buf.at[b], ag_r.at[i, b], on_ctx(2))
        send(buf.at[b], buf.at[b], ag_s.at[i, 2], ag_r.at[i, b], on_ctx(1))

    def ag_wait(i, buf, d):
        arrived(buf.at[rel(d)], ag_r.at[i, rel(d)], on_ctx(d))

    def rs_put(i, d, h, val):
        cols = pl.ds(h * half_w, half_w)
        if d == 0:
            keep[:, cols] = val
            return
        k = {3: 0, 2: 1, 1: 2}[d]
        if d == 2:
            arrived(land.at[i, 0, h], rs_r.at[i, 0, h], on_ctx(1))
            val = val + land[i, 0, h].astype(F32)
        snd[i % 2, k, h] = val.astype(BF16)
        make(snd.at[i % 2, k, h], land.at[i, k, h], rs_s.at[i, k, h], rs_r.at[i, k, h], on_ctx(2 if d == 2 else 1)).start()

    def rs_sent(i):
        for d, k in ((3, 0), (2, 1), (1, 2)):
            for h in range(2):
                make(snd.at[i % 2, k, h], land.at[i, k, h], rs_s.at[i, k, h], rs_r.at[i, k, h],
                     on_ctx(2 if d == 2 else 1)).wait_send()

    def rs_arrived(i):
        for h in range(2):
            arrived(land.at[i, 2, h], rs_r.at[i, 2, h], on_ctx(1))
            arrived(land.at[i, 1, h], rs_r.at[i, 1, h], on_ctx(2))

    def rs_rows(i, rw):
        parts = [keep[rw, pl.ds(h * half_w, half_w)] + land[i, 1, h, rw].astype(F32) + land[i, 2, h, rw].astype(F32)
                 for h in range(2)]
        return jnp.concatenate(parts, 1)

    def chunks(fn, init=0, size=CHUNK):
        return lax.fori_loop(0, t_rows // size, lambda i, v: fn(pl.ds(pl.multiple_of(i * size, size), size), v), init)

    sg = seg[...]
    start = jnp.zeros_like(sg)
    for doc in range(DOCS - 1):
        start = start + jnp.where(sg > doc, jnp.sum((sg == doc).astype(jnp.int32), -1, keepdims=True), 0)
    for b in range(n):
        start_s[b] = start[:, b * t_rows:(b + 1) * t_rows]

    local_done(wo.at[:, f], loc.at[2])
    w_own(OUT, 0)
    local_done(wb.at[:, f], loc.at[4])
    w_own(BACK, 0)
    for d in (1, 2, 3):
        arrived(packs.at[rel(d), f], pk_cr.at[rel(d)], on_ctx(d))
    for s in range(1, nf):
        f2 = (f + s) % nf
        send(packs.at[:, f], packs.at[:, f], pk_zs.at[s], pk_zr.at[f], on_z(f2))
    local_done(wq.at[:, c, f], loc.at[1])
    exchanged(0, wq)
    w_own(QKV, 0)
    w_own(QKV, 1)
    w_swap(OUT, 0, 1)
    w_swap(BACK, 0, 1)
    for s in range(1, nf):
        f2 = (f + s) % nf
        arrived(packs.at[:, f2], pk_zr.at[f2], on_z(f2))
    lane = lax.broadcasted_iota(jnp.int32, (8, 128), 1)
    per = 128 // rows
    for g in range(width // 128):
        acc = None
        for j in range(per):
            e = g * per + j
            piece = packs[e // nf, e % nf].astype(F32)[0:8]
            acc = piece if j == 0 else jnp.where(lane // rows == j, pltpu.roll(piece, j * rows, 1), acc)
        vecs[g] = acc
    for g in range(ffc // 128):
        acc = None
        for j in range(per):
            e = g * per + j
            k = e % 4
            piece = packs[c, e // 4].astype(F32)[8:16]
            piece = jnp.broadcast_to(piece[k:k + 1], (8, 128))
            acc = piece if j == 0 else jnp.where(lane // rows == j, pltpu.roll(piece, j * rows, 1), acc)
        inb[:, g * 128:(g + 1) * 128] = acc

    def vec(v):
        return jnp.concatenate([vecs[g, v:v + 1, :] for g in range(width // 128)], 1)

    def ln1(rw, _):
        z, _r = norm_parts(tok[rw].astype(F32))
        n1[c, rw] = (z * vec(0) + vec(1)).astype(BF16)
        return 0
    chunks(ln1)
    ag_start(0, n1)
    local_done(cot.at[c], loc.at[0])
    ag_start(1, cot)
    w_step(QKV, 0, 1)
    w_step(QKV, 1, 1)
    w_relay(OUT, 0)
    local_done(wi.at[:, c, f], loc.at[3])
    exchanged(1, wi)
    w_own(IN, 0)
    w_own(IN, 1)
    w_relay(BACK, 0)
    for s in (3, 2):
        w_step(QKV, 0, s)
        w_step(QKV, 1, s)
    w_step(OUT, 0, 3)
    w_step(OUT, 0, 2)
    ag_forward(0, n1)
    ag_wait(0, n1, 1)
    ag_wait(0, n1, 3)
    w_arrived(QKV)

    def project(b, _):
        for p in range(2):
            pr = dot(n1[b], wq[p].reshape(width, 3 * pw), NN)
            qv = ((pr[:, :pw] + vecs[c * 2 + p, 2:3, :]).astype(BF16).astype(F32) * (HD ** -0.5)).astype(BF16)
            kv = pr[:, pw:2 * pw].astype(BF16)
            vv = (pr[:, 2 * pw:] + vecs[c * 2 + p, 3:4, :]).astype(BF16)
            kt, vt = kv.T, vv.T
            for e in range(2):
                q_s[2 * p + e, b] = qv[:, e * HD:(e + 1) * HD]
                k_s[2 * p + e, b] = kv[:, e * HD:(e + 1) * HD]
                v_s[2 * p + e, b] = vv[:, e * HD:(e + 1) * HD]
                kt_s[2 * p + e, b] = kt[e * HD:(e + 1) * HD]
                vt_s[2 * p + e, b] = vt[e * HD:(e + 1) * HD]
        return 0
    lax.fori_loop(0, n, project, 0)

    key_row = lax.broadcasted_iota(jnp.int32, (t_rows, t_rows), 0)
    query_col = lax.broadcasted_iota(jnp.int32, (t_rows, t_rows), 1)

    def allowed(qb, kb, diagonal):
        ok = key_row >= start_s[qb] - kb * t_rows
        return ok & (key_row <= query_col) if diagonal else ok

    def scores(h, qb, kb, ok):
        return jnp.where(ok, dot(k_s[h, kb], q_s[h, qb], NT), MASKED)

    def attend(heads, qb):
        def step(kb, carry, diagonal=False):
            ok = allowed(qb, kb, diagonal)
            out = []
            for h, (m, l, acc) in zip(heads, carry):
                s = scores(h, qb, kb, ok)
                m2 = jnp.maximum(m, jnp.max(s, 0, keepdims=True))
                p = jnp.exp(s - m2)
                a = jnp.exp(m - m2)
                out.append((m2, l * a + jnp.sum(p, 0, keepdims=True), acc * a + dot(vt_s[h, kb], p.astype(BF16), NN)))
            return tuple(out)
        zero = jnp.zeros((1, t_rows), F32)
        carry = lax.fori_loop(0, qb, step, tuple((zero + MASKED, zero, jnp.zeros((HD, t_rows), F32)) for _ in heads))
        for h, (m, l, acc) in zip(heads, step(qb, carry, True)):
            att[qb, h] = (acc / l).astype(BF16)
            lse_s[h, qb] = m + jnp.log(l)

    polls = [[(IN, 0, 1), (BACK, 0, 3)], [(IN, 1, 1)], [(IN, 0, 3), (BACK, 0, 2)], [(IN, 1, 3)], [(IN, 0, 2)], [(IN, 1, 2)],
             [(BACK, 1, 1)], [(BACK, 1, 3)]]
    for d in (3, 2, 1, 0):
        qb = rel(d)
        for k in range(2):
            attend((2 * k, 2 * k + 1), qb)
            for poll in polls[2 * (3 - d) + k]:
                w_step(*poll)
            if d == 3 and k == 1:
                w_own(BACK, 1)
        if d == 3:
            w_arrived(OUT)
        if d == 2:
            ag_forward(1, cot)
        for h in range(2):
            rs_put(0, d, h, dot(att[qb].reshape(hc, t_rows), wo[h].reshape(hc, half_w), TN))
    rs_arrived(0)

    def ln2(rw, _):
        res = tok[rw].astype(F32) + rs_rows(0, rw) + vec(4)
        resid[rw] = res
        z, _r = norm_parts(res)
        n2[c, rw] = (z * vec(5) + vec(6)).astype(BF16)
        return 0
    chunks(ln2)
    ag_start(2, n2)
    w_step(BACK, 1, 2)
    w_arrived(IN)

    for d in (0, 1, 3, 2):
        b = rel(d)
        if d == 1:
            ag_wait(2, n2, 1)
        if d == 3:
            ag_forward(2, n2)
            ag_wait(2, n2, 3)

        def up(j, _):
            tmp1[...] = dot(n2[b], wi[j].reshape(width, half_f), NN)
            cols = pl.ds(pl.multiple_of(j * half_f, half_f), half_f)
            bias = inb[0:1, cols]

            def one(rw, _):
                a, da = gelu_both(tmp1[rw] + bias)
                act[b, rw, cols] = a.astype(BF16)
                gpre[b, rw, cols] = da.astype(BF16)
                return 0
            chunks(one)
            return 0
        lax.fori_loop(0, 2, up, 0)
    rs_sent(0)
    ag_wait(1, cot, 1)
    ag_wait(1, cot, 3)

    grads = {OUT: (gwo, yo, zo), IN: (gwi, yi, zi), BACK: (gwb, yb, zb)}
    alls = {QKV: aq.at[0], LATE: aq.at[1], OUT: ao, IN: ai, BACK: ab}
    nh = n // 2

    def g_part(kind, r2, f2):
        if kind in (QKV, LATE):
            return gwq.at[kind // LATE, pl.ds(r2 * nh, nh), f2]
        return block(grads[kind][0], kind, r2, f2)

    def y_part(kind, f2):
        if kind in (QKV, LATE):
            return yq.at[kind // LATE, :, f2]
        return grads[kind][1].at[:, f2] if kind == IN else grads[kind][1].at[f2]

    def z_part(kind, f2):
        return zq.at[kind // LATE, f2] if kind in (QKV, LATE) else grads[kind][2].at[f2]

    def g_y(kind):
        for s in (*range(1, nf), 0):
            f2 = (f + s) % nf
            send(g_part(kind, 1 - r, f2), y_part(kind, f2), gy_s.at[kind, f2], gy_r.at[kind, f2], on_y)

    def g_z(kind, s):
        f2 = (f + s) % nf
        g, y = g_part(kind, r, f2), y_part(kind, f2)
        arrived(y, gy_r.at[kind, f2], on_y)
        if kind in (OUT, BACK):
            g[...] = (g[...].astype(F32) + y[...].astype(F32)).astype(BF16)
        else:
            for i in range(y.shape[0]):
                g[i] = (g[i].astype(F32) + y[i].astype(F32)).astype(BF16)
        if s:
            send(g, z_part(kind, f), gz_s.at[kind, s], gz_r.at[kind, f], on_z(f2))

    def g_rest(kind, s0):
        for s in (*range(s0, nf), 0):
            g_z(kind, s)

    def g_f(kind):
        for s in range(1, nf):
            f2 = (f + s) % nf
            arrived(z_part(kind, f2), gz_r.at[kind, f2], on_z(f2))
        g = g_part(kind, r, f)
        zs = [z_part(kind, (f + s) % nf) for s in range(1, nf)]
        if kind in (OUT, BACK):
            tot = g[...].astype(F32)
            for z in zs:
                tot = tot + z[...].astype(F32)
            alls[kind][r] = tot.astype(BF16)
            send(alls[kind].at[r], alls[kind].at[r], gf_s.at[kind], gf_r.at[kind], on_y)
            return
        fin = fi if kind == IN else fq.at[kind // LATE]
        for i in range(fin.shape[0]):
            tot = g[i].astype(F32)
            for z in zs:
                tot = tot + z[i].astype(F32)
            fin[i] = tot.astype(BF16)
        if kind == IN:
            for d in (2, 3, 1):
                send(fin.at[rel(d)], ai.at[r, c], gc_s.at[kind, d], gc_r.at[kind, c], on_ctx(d))
            ai[r, c] = fin[c]
            return
        for i in range(nh):
            owner = r * nh + i
            send(fin.at[i], alls[kind].at[c], gc_s.at[kind, i], gc_r.at[kind, c], (owner, f, r), owner != c)

            @pl.when(owner == c)
            def _():
                alls[kind][c] = fin[i]

    def g_e(kind):
        a = alls[kind]
        if kind == IN:
            for d in (1, 2, 3):
                arrived(a.at[r, rel(d)], gc_r.at[kind, rel(d)], on_ctx(d))
            send(a.at[r], a.at[r], gf_s.at[kind], gf_r.at[kind], on_y)
            return

        @pl.when(c // nh == r)
        def _():
            for d in (1, 2, 3):
                arrived(a.at[rel(d)], gc_r.at[kind, rel(d)], on_ctx(d))
        send(a, a, gf_s.at[kind], gf_r.at[kind], on_y, c // nh == r)

    def g_out(kind):
        a = alls[kind]
        if kind in (QKV, LATE):
            @pl.when(c // nh != r)
            def _():
                arrived(a, gf_r.at[kind], on_y)
            h = kind // LATE
            for c2 in range(n):
                for j in range(3):
                    local(a.at[c2, :, pl.ds(j * pw, pw)], gq_o.at[:, pl.ds(j * width + c2 * hc + h * pw, pw)], out_s.at[kind])
            return
        arrived(a.at[1 - r], gf_r.at[kind], on_y)
        for h in range(2):
            if kind == IN:
                for c2 in range(n):
                    local(a.at[h, c2], gi_o.at[:, pl.ds(c2 * ffc + h * half_f, half_f)], out_s.at[kind])
            else:
                local(a.at[h], (go_o if kind == OUT else gb_o).at[:, pl.ds(h * half_w, half_w)], out_s.at[kind])

    def whole(buf, cols):
        v = buf[:, :, cols]
        return v.reshape(n * t_rows, v.shape[2])

    def grad_back(h):
        per_f = ffc // nf
        tiles = max(1, 256 // per_f)

        def one(i, _):
            a = whole(act, pl.ds(pl.multiple_of(i * 256, 256), 256))
            g = whole(cot, pl.ds(pl.multiple_of(h * half_w, half_w), half_w))
            v = dot(a, g, TN).astype(BF16)
            gwb[h, pl.ds(i * tiles, tiles)] = v.reshape(tiles, per_f, half_w)
            return 0
        lax.fori_loop(0, ffc // 256, one, 0)

    def grad_in(h):
        def one(i, _):
            a = whole(n2, pl.ds(pl.multiple_of(i * hc, hc), hc))
            g = whole(gpre, pl.ds(pl.multiple_of(h * half_f, half_f), half_f))
            gwi[h, i] = dot(a, g, TN).astype(BF16).reshape(nf, rows, half_f)
            return 0
        lax.fori_loop(0, n, one, 0)

    grad_back(1 - r)
    g_y(BACK)
    grad_back(r)
    w_arrived(BACK)

    ibg[...] = jnp.zeros_like(ibg)
    for d in (3, 2, 1, 0):
        b = rel(d)

        def slope(j, _):
            wide = jnp.concatenate([wb[h, pl.ds(j * (nf // 2), nf // 2)].reshape(half_f, half_w) for h in range(2)], 1)
            tmp2[...] = dot(cot[b], wide, NT)
            cols = pl.ds(pl.multiple_of(j * half_f, half_f), half_f)

            def one(rw, acc):
                gp = (tmp2[rw] * gpre[b, rw, cols].astype(F32)).astype(BF16)
                gpre[b, rw, cols] = gp
                return acc + fold(gp.astype(F32))
            ibg[j] += chunks(one, jnp.zeros((8, half_f), F32))
            return 0
        lax.fori_loop(0, 2, slope, 0)
        for h in range(2):
            wide = jnp.concatenate([wi[j, pl.ds(h * (n // 2), n // 2)].reshape(half_w, half_f) for j in range(2)], 1)
            rs_put(1, d, h, dot(gpre[b], wide, NT))
    grad_in(1 - r)
    g_y(IN)
    g_z(BACK, 1)
    grad_in(r)
    rs_arrived(1)

    def ln2_back(rw, accs):
        gain, shift, bb, ob = accs
        g = rs_rows(1, rw)
        z, rstd = norm_parts(resid[rw])
        ct = cot[c, rw].astype(F32)
        gr = ct + norm_back(g, z, rstd, vec(5))
        gres[rw] = gr
        low = gr.astype(BF16)
        gbr[c, rw] = low
        return gain + fold(g * z), shift + fold(g), bb + fold(ct), ob + fold(low.astype(F32))
    zero8 = jnp.zeros((8, width), F32)
    accs = chunks(ln2_back, (zero8, zero8, zero8, zero8), 16)
    for i, a in zip((3, 4, 5, 2), accs):
        sums[i] = a
    ag_start(3, gbr)
    if nf > 2:
        g_z(BACK, 2)

    for d in (3, 2, 1, 0):
        for h in range(2):
            rs_put(2, d, h, dot(act[rel(d)], wb[h].reshape(ffc, half_w), NN))
    ag_wait(3, gbr, 1)

    def near(t):
        return rel(t ^ (t // 2))

    def g_attended(t, _):
        b = near(t)
        wide = jnp.concatenate([wo[h].reshape(hc, half_w) for h in range(2)], 1)
        g = dot(gbr[b], wide, NT).astype(BF16)
        gt = g.T.astype(F32).reshape(H // n, HD, t_rows)
        for h in range(H // n):
            do_s[h, b] = g[:, h * HD:(h + 1) * HD]
            delta_s[h, b] = jnp.sum(gt[h] * att[b, h].astype(F32), 0, keepdims=True)
        return 0
    lax.fori_loop(0, 2, g_attended, 0)

    def grad_out(h):
        tot = jnp.zeros((hc, half_w), F32)
        cols = pl.ds(pl.multiple_of(h * half_w, half_w), half_w)
        for b in range(n):
            tot = tot + dot(att[b].reshape(hc, t_rows), gbr[b, :, cols], NN)
        gwo[h] = tot.astype(BF16).reshape(nf, rows, half_w)

    def finish_out(rw, _):
        out_o[rw] = (resid[rw] + rs_rows(2, rw) + vec(7)).astype(BF16)
        return 0

    def pair_blocks(p, lo, hi):
        def one(t, _):
            qb = near(t)

            def step(kb, dqts, diagonal=False):
                ok = allowed(qb, kb, diagonal)
                out = []
                for e in range(2):
                    h = 2 * p + e
                    q, do = q_s[h, qb], do_s[h, qb]
                    pr = jnp.exp(scores(h, qb, kb, ok) - lse_s[h, qb])
                    dp = dot(v_s[h, kb], do, NT)
                    ds = (pr * (dp - delta_s[h, qb])).astype(BF16)
                    dv_s[e, kb] += dot(pr.astype(BF16), do, NN)
                    dk_s[e, kb] += dot(ds, q, NN)
                    out.append(dqts[e] + dot(kt_s[h, kb], ds, NN))
                return tuple(out)
            dqts = lax.fori_loop(0, qb, step, (jnp.zeros((HD, t_rows), F32),) * 2)
            for e, dqt in enumerate(step(qb, dqts, True)):
                gproj[p, qb, :, e * HD:(e + 1) * HD] = (dqt * (HD ** -0.5)).T.astype(BF16)
            return 0
        lax.fori_loop(lo, hi, one, 0)

    def pair_start():
        dk_s[...] = jnp.zeros_like(dk_s)
        dv_s[...] = jnp.zeros_like(dv_s)

    def pair_end(p):
        for e in range(2):
            for b in range(n):
                gproj[p, b, :, pw + e * HD:pw + (e + 1) * HD] = dk_s[e, b].astype(BF16)
                gproj[p, b, :, 2 * pw + e * HD:2 * pw + (e + 1) * HD] = dv_s[e, b].astype(BF16)

        def grad_qkv(i, _):
            a = whole(n1, pl.ds(pl.multiple_of(i * hc, hc), hc))
            gwq[p, i] = dot(a, gproj[p].reshape(n * t_rows, 3 * pw), TN).astype(BF16).reshape(nf, rows, 3 * pw)
            return 0
        lax.fori_loop(0, n, grad_qkv, 0)

    pair_start()
    pair_blocks(0, 0, 2)
    g_rest(BACK, 3)
    ag_forward(3, gbr)
    ag_wait(3, gbr, 3)
    g_z(IN, 1)
    lax.fori_loop(2, n, g_attended, 0)
    pair_blocks(0, 2, 3)
    if nf > 2:
        g_z(IN, 2)
    pair_blocks(0, 3, n)
    for s in range(3, nf):
        g_z(IN, s)
    pair_end(0)
    g_y(QKV)
    g_z(IN, 0)
    grad_out(1 - r)
    g_y(OUT)
    grad_out(r)
    rs_arrived(2)
    chunks(finish_out)
    pair_start()
    pair_blocks(1, 0, 2)
    g_z(QKV, 1)
    if nf > 2:
        g_z(QKV, 2)
    pair_blocks(1, 2, n)
    pair_end(1)
    g_y(LATE)
    g_rest(QKV, 3)
    rs_sent(1)
    for d in (3, 2, 1, 0):
        for h in range(2):
            gp = jnp.concatenate([gproj[p, rel(d)] for p in range(2)], 1)
            wide = jnp.concatenate([wq[p, pl.ds(h * (n // 2), n // 2)].reshape(half_w, 3 * pw) for p in range(2)], 1)
            rs_put(3, d, h, dot(gp, wide, NT))
    g_f(IN)
    g_f(BACK)
    g_rest(OUT, 1)
    g_rest(LATE, 1)
    g_f(QKV)
    g_e(IN)
    rs_arrived(3)

    def ln1_back(rw, accs):
        gain, shift = accs
        g = rs_rows(3, rw)
        z, rstd = norm_parts(tok[rw].astype(F32))
        gx_o[rw] = gres[rw] + norm_back(g, z, rstd, vec(0))
        return gain + fold(g * z), shift + fold(g)
    accs = chunks(ln1_back, (zero8, zero8), 16)
    sums[0], sums[1] = accs[0], accs[1]

    g_e(QKV)
    g_f(OUT)
    for i in range(8):
        row = jnp.sum(sums[i], 0, keepdims=True) if i < 6 else jnp.zeros((1, width), F32)
        for c2 in range(n):
            v6[c2, i:i + 1, :] = row[:, c2 * hc:(c2 + 1) * hc]
    for d in (1, 2, 3):
        send(v6.at[rel(d)], v6r.at[c], vc_s.at[d], vc_r.at[c], on_ctx(d))
    vs[...] = jnp.zeros_like(vs)
    for p in range(2):
        gsum = jnp.sum(gproj[p].reshape(n * t_rows, 3 * pw).astype(F32), 0, keepdims=True)
        v6[c, 6:7, p * pw:(p + 1) * pw] = gsum[:, :pw]
        v6[c, 7:8, p * pw:(p + 1) * pw] = gsum[:, 2 * pw:]
    for j in range(2):
        row = jnp.sum(ibg[j], 0, keepdims=True)
        for k in range(2):
            i = 8 + 2 * j + k
            vs[i:i + 1, :] = row[:, k * hc:(k + 1) * hc]
    for d in (1, 2, 3):
        arrived(v6r.at[rel(d)], vc_r.at[rel(d)], on_ctx(d))
    vs[0:8] = v6[c] + v6r[rel(1)] + v6r[rel(2)] + v6r[rel(3)]
    me = r * nf + f
    vz[me] = vs[...]
    for k in range(1, 2 * nf):
        f2, r2 = (f + k) % nf, (r + k // nf) % 2
        send(vs, vz.at[me], vz_s.at[k], vz_r.at[me], (c, f2, r2))
    g_f(LATE)
    g_e(LATE)
    g_out(BACK)
    g_out(OUT)
    for k in range(1, 2 * nf):
        f2, r2 = (f + k) % nf, (r + k // nf) % 2
        arrived(vz.at[r2 * nf + f2], vz_r.at[r2 * nf + f2], (c, f2, r2))
    tot = vz[0]
    for k in range(1, 2 * nf):
        tot = tot + vz[k]
    mine, mine_in = tot[:, :rows], tot[8:9, :4 * rows]
    for f2 in range(1, nf):
        row, lo = 8 + f2 * 4 * rows // hc, f2 * 4 * rows % hc
        mine = jnp.where(f == f2, tot[:, f2 * rows:(f2 + 1) * rows], mine)
        mine_in = jnp.where(f == f2, tot[row:row + 1, lo:lo + 4 * rows], mine_in)
    gv_o[0:16, :rows] = mine
    gv_o[16:17, :4 * rows] = mine_in
    g_out(IN)
    g_out(QKV)
    g_out(LATE)
    rs_sent(2)
    rs_sent(3)
    for end in ends:
        end()
    for kind in range(5):
        local_done(alls[kind], out_s.at[kind])


def finish(lo_i, gx_i, gq_i, go_i, gi_i, gb_i, lo_o, gx_o, gq_o, go_o, gi_o, gb_o,
           lo_b, gx_b, gq_b, go_b, gi_b, gb_b, gq_w, go_w, gi_w, gb_w, sem_i, sem_o):
    parts = [(gb_i, gb_b, gb_w, gb_o), (gi_i, gi_b, gi_w, gi_o), (gq_i, gq_b, gq_w, gq_o), (go_i, go_b, go_w, go_o),
             (gx_i, gx_b, gx_b, gx_o), (lo_i, lo_b, lo_b, lo_o)]
    for k, (src, low, wide, dst) in enumerate(parts):
        pltpu.make_async_copy(src, low, sem_i.at[k]).start()
    for k, (src, low, wide, dst) in enumerate(parts):
        pltpu.make_async_copy(src, low, sem_i.at[k]).wait()
        if wide is not low:
            wide[...] = low[...].astype(F32)
        pltpu.make_async_copy(wide, dst, sem_o.at[k]).start()
    for k, (src, low, wide, dst) in enumerate(parts):
        pltpu.make_async_copy(wide, dst, sem_o.at[k]).wait()


def shards(n, nf, tokens, segments, ln1_gain, ln1_bias, w_qkv, q_bias, v_bias, w_out, out_bias,
           ln2_gain, ln2_bias, w_in, in_bias, w_back, back_bias, cotangent):
    t_rows, width = tokens.shape[1], tokens.shape[2]
    rows, brows = w_qkv.shape[0], w_back.shape[0]
    ffc = w_in.shape[1] // n
    slots = segments.shape[1]
    heads = H // n
    hc, half_w, half_f = width // n, width // 2, ffc // 2
    q3 = 3 * hc // 2
    small = jnp.stack([ln1_gain, ln1_bias, q_bias, v_bias, out_bias, ln2_gain, ln2_bias, back_bias])
    small = jnp.concatenate([small, in_bias.reshape(4, rows), jnp.zeros((4, rows), BF16)], 0)
    small = jnp.pad(small, ((0, 0), (0, 128 - rows)))
    dims = (n, nf, t_rows, width, rows, brows, ffc)
    vm = pltpu.VMEM
    dma = pltpu.SemaphoreType.DMA
    per_head = (heads, n, t_rows, HD)
    per_head_t = (heads, n, HD, t_rows)
    scratch = [
        vm((2, n, nf, rows, q3), BF16), vm((2, nf, rows, half_w), BF16), vm((2, n, nf, rows, half_f), BF16),
        vm((2, nf, brows, half_w), BF16), vm((n, nf, 16, 128), BF16), vm((width // 128, 8, 128), F32), vm((8, ffc), F32),
        vm((n, t_rows, width), BF16), vm((n, t_rows, width), BF16), vm((n, t_rows, width), BF16), vm((n, t_rows, width), BF16),
        vm(per_head, BF16), vm(per_head, BF16), vm(per_head, BF16), vm(per_head, BF16), vm(per_head_t, BF16), vm(per_head_t, BF16),
        vm((n, heads, HD, t_rows), BF16), vm((n, t_rows, ffc), BF16), vm((n, t_rows, ffc), BF16), vm((2, n, t_rows, q3), BF16),
        vm((n, 1, t_rows), jnp.int32), vm((heads, n, 1, t_rows), F32), vm((heads, n, 1, t_rows), F32),
        vm((t_rows, width), F32), vm((t_rows, width), F32), vm((t_rows, width), F32), vm((t_rows, half_f), F32), vm((t_rows, half_f), F32),
        vm((2, 3, 2, t_rows, half_w), BF16), vm((4, 3, 2, t_rows, half_w), BF16),
        vm((2, n, t_rows, HD), F32), vm((2, n, t_rows, HD), F32),
        vm((2, n, nf, rows, q3), BF16), vm((2, nf, rows, half_w), BF16), vm((2, n, nf, rows, half_f), BF16), vm((2, nf, brows, half_w), BF16),
        vm((2, n // 2, nf, rows, q3), BF16), vm((nf, rows, half_w), BF16), vm((n, nf, rows, half_f), BF16), vm((nf, brows, half_w), BF16),
        vm((2, nf, n // 2, rows, q3), BF16), vm((nf, rows, half_w), BF16), vm((nf, n, rows, half_f), BF16), vm((nf, brows, half_w), BF16),
        vm((2, n // 2, rows, q3), BF16), vm((n, rows, half_f), BF16),
        vm((2, n, rows, q3), BF16), vm((2, rows, half_w), BF16), vm((2, n, rows, half_f), BF16), vm((2, brows, half_w), BF16),
        vm((n, 8, hc), F32), vm((n, 8, hc), F32), vm((16, hc), F32), vm((2 * nf, 16, hc), F32),
        vm((2, 8, half_f), F32), vm((8, 8, width), F32),
        dma((5,)), dma((4,)), dma((n,)), dma((nf,)), dma((nf,)), dma((2, 4)), dma((2, n)),
        dma((4, 2, 4 + 2 * max(0, nf - 3))), dma((4, 2, nf)), dma((4, 2, nf)), dma((4, 2, nf)), dma((4, 3)), dma((4, n)), dma((4, 3, 2)), dma((4, 3, 2)),
        dma((5, nf)), dma((5, nf)), dma((5, nf)), dma((5, nf)), dma((5, 4)), dma((5, n)), dma((5,)), dma((5,)),
        dma((4,)), dma((n,)), dma((2 * nf,)), dma((2 * nf,)), dma((5,)),
    ]
    shape = jax.ShapeDtypeStruct
    in_vmem, in_hbm = pl.BlockSpec(memory_space=vm), pl.BlockSpec(memory_space=pl.ANY)
    outs = pl.pallas_call(
        functools.partial(body, dims),
        out_shape=[shape((t_rows, width), BF16), shape((t_rows, width), F32), shape(w_qkv.shape, BF16), shape(w_out.shape, BF16),
                   shape(w_in.shape, BF16), shape(w_back.shape, BF16), shape((24, hc), F32)],
        in_specs=[in_vmem, in_hbm, in_vmem, in_vmem] + [in_hbm] * 4,
        out_specs=[in_vmem] * 2 + [in_hbm] * 4 + [in_vmem],
        scratch_shapes=scratch,
        compiler_params=pltpu.CompilerParams(collective_id=0, has_side_effects=True, vmem_limit_bytes=67043328),
    )(tokens[0], cotangent[0], segments, small, w_qkv, w_out, w_in, w_back)
    gv = outs[6]
    grads = [w_qkv, w_out, w_in, w_back]
    layer_output, input_grad, g_qkv, g_out, g_in, g_back = pl.pallas_call(
        finish,
        out_shape=[shape((t_rows, width), BF16), shape((t_rows, width), F32)] + [shape(g.shape, F32) for g in grads],
        in_specs=[in_hbm] * 6,
        out_specs=[in_hbm] * 6,
        scratch_shapes=[vm((t_rows, width), BF16), vm((t_rows, width), F32)] + [vm(g.shape, BF16) for g in grads]
        + [vm(g.shape, F32) for g in grads] + [dma((6,)), dma((6,))],
    )(*outs[:6])
    mine = gv[:8, :rows]
    return (layer_output[None], input_grad[None], mine[0], mine[1], g_qkv, mine[6], mine[7], g_out,
            mine[2], mine[3], mine[4], g_in, gv[16, :4 * rows], g_back, mine[5])


def solution(mesh):
    both = ("ctx", "fsdp")
    own, rows = P(both), P(both, None)
    seqs = P(("fsdp", "rep"), "ctx", None)
    in_specs = (seqs, P(("fsdp", "rep"), None), own, own, rows, own, own, rows, own, own, own, rows, own, rows, own, seqs)
    out_specs = (seqs, seqs, own, own, rows, own, own, rows, own, own, own, rows, own, rows, own)
    run = functools.partial(shards, mesh.shape["ctx"], mesh.shape["fsdp"])
    return jax.shard_map(run, mesh=mesh, in_specs=in_specs, out_specs=out_specs, check_vma=False)
```
